256 devices in a mesh: tm: 64 (over y, x_hi, z), space: 4 (over x_lo, core).
Axes of the slice: x: 4 (x_hi: 2, x_lo: 2; x = x_hi * 2 + x_lo), y: 4, z: 8, core: 2. Of those that a mesh axis runs over, the one named last changes fastest.
Arguments:
- states: float32 [64, 3, 256, 1024], P('tm', None, 'space'), may hold values from -3 to 3
- background: float32 [3, 256, 1024], P(None, 'space'), may hold values from -3 to 3
- obs_cells: int32 [64, 4, 1024], P('tm'), may hold values from 0 to 262143
- obs_values: float32 [64, 4, 1024], P('tm'), may hold values from -3 to 3
- land_mask: int32 [256, 1024], P('space'), may hold values 0 or 1
Outputs:
- gradient: float32 [64, 3, 256, 1024], P('tm', None, 'space')
- next_states: float32 [64, 3, 256, 1024], P('tm', None, 'space')
The draws below stay inside these ranges and needn't reach their ends.
All inputs are finite; a program needn't handle non-finite values. No bound on the sum of `land_mask` on one device may be relied on, other than what follows from the above.
Results may differ from the reference program's by a relative error of at most 0.0003.
Values sent between devices are 32-bit elements; how exact they have to be, the bound alone decides.
No kernel may reach another device: no remote copies, remote signals or barrier semaphores. Data moves between devices by JAX's collectives and lax.ppermute only.
A program may use at most 64 MiB of HBM per device.

```python
import jax
import jax.numpy as jnp
from jax import lax

NLON = 1024
NSTEP = 4
OBS = 1024
NY = 256
SUBWIN = 64


def place_ends(array, rng, least, high):
    index_at = [jax.random.randint(jax.random.fold_in(rng, axis), (), 0, length) for axis, length in enumerate(array.shape)]
    main_axis = array.shape.index(max(array.shape))
    beside = index_at[:main_axis] + [(index_at[main_axis] + 1) % array.shape[main_axis]] + index_at[main_axis + 1:]
    return array.at[tuple(index_at)].set(least).at[tuple(beside)].set(high)


def shard_levels(key, extent, shards, least, top_value):
    def one(axis_at, blocks):
        steps = jax.random.uniform(jax.random.fold_in(jax.random.fold_in(key, 6), axis_at), (blocks,), jnp.float32, least / len(shards), top_value / len(shards))
        return jnp.repeat(jnp.exp(steps), extent[axis_at] // blocks).reshape((-1,) + (1,) * (len(extent) - axis_at - 1))

    factor_of = one(*shards[0])
    for cut in shards[1:]:
        factor_of = factor_of * one(*cut)
    return factor_of


def bell_draw(own_key, shape, width, reach, split=(), dtype=jnp.bfloat16):
    gain = shard_levels(own_key, shape, split, -0.22, 0.18) if split else 1.0
    array = jax.random.normal(own_key, shape, jnp.float32) * width * gain
    return jnp.minimum(jnp.maximum(array, -reach), reach).astype(dtype)


def setup_inputs(seed: int = 0) -> dict:
    arg_keys = jax.random.split(jax.random.key(seed), 6)
    states = bell_draw(arg_keys[0], (SUBWIN, 3, NY, NLON), 0.5, 3.0, ((0, 64), (2, 4)), jnp.float32)
    background = bell_draw(arg_keys[1], (3, NY, NLON), 0.5, 3.0, ((1, 4),), jnp.float32)
    obs_cells = place_ends(jax.random.randint(arg_keys[2], (SUBWIN, NSTEP, OBS), 0, NY * NLON), jax.random.fold_in(arg_keys[2], 1), 0, (NY * NLON) - 1).astype(jnp.int32)
    obs_values = bell_draw(arg_keys[3], (SUBWIN, NSTEP, OBS), 0.5, 3.0, ((0, 64),), jnp.float32)
    land_mask = place_ends((jax.random.randint(arg_keys[4], (NY, NLON), 0, 5) < 4).astype(jnp.int32), jax.random.fold_in(arg_keys[4], 1), 0, 1)
    return dict(states=states, background=background, obs_cells=obs_cells, obs_values=obs_values, land_mask=land_mask)


advect = 0.25
gravity = 1.0
coriolis = 0.1
diffuse = 0.1
defect_weight = 2.0
obs_weight = 4.0
step_length = 0.1

def along_lon(field):
    return (jnp.roll(field, -1, axis=-1) - jnp.roll(field, 1, axis=-1)) / 2.0

def advance(padded, land):
    height, zonal, merid = (padded[0], padded[1], padded[2])
    flux_x = (1.0 + height) * zonal
    flux_y = (1.0 + height) * merid

    def laplace(field):
        inner = field[1:-1]
        return field[2:] + field[:-2] + jnp.roll(inner, 1, axis=-1) + jnp.roll(inner, -1, axis=-1) - 4.0 * inner
    diverge = along_lon(flux_x)[1:-1] + (flux_y[2:] - flux_y[:-2]) / 2.0
    h_inner, u_inner, v_inner = (height[1:-1], zonal[1:-1], merid[1:-1])
    h_new = h_inner - advect * diverge + diffuse * laplace(height)
    u_new = land * (u_inner - advect * gravity * along_lon(height)[1:-1] + coriolis * v_inner + diffuse * laplace(zonal))
    v_new = land * (v_inner - advect * gravity * (height[2:] - height[:-2]) / 2.0 - coriolis * u_inner + diffuse * laplace(merid))
    return jnp.stack([h_new, u_new, v_new])

def subwindow(state, cells, values, land):
    current = state
    misfits = []
    for step in range(NSTEP):
        current = advance(jnp.pad(current, ((0, 0), (1, 1), (0, 0))), land)
        seen = jnp.take(current[0].reshape(-1), cells[step].astype(jnp.int32))
        misfits.append(seen - values[step])
    return (current, jnp.stack(misfits))

def reference(states, background, obs_cells, obs_values, land_mask):
    land = land_mask.astype(jnp.float32)
    ends = lax.map(lambda group: subwindow(group[0], group[1], group[2], land)[0], (states, obs_cells, obs_values))
    previous = jnp.concatenate([background[None], ends[:-1]], axis=0)
    defects = states - previous
    following = jnp.concatenate([defects[1:], jnp.zeros_like(defects[:1])], axis=0)

    def adjoint(group):
        state, cells, values, ahead = group
        outputs, pullback = jax.vjp(lambda s: subwindow(s, cells, values, land), state)
        return pullback((-defect_weight * ahead, obs_weight * outputs[1]))[0]
    gradient = defect_weight * defects + lax.map(adjoint, (states, obs_cells, obs_values, following))
    updated = states - step_length * gradient
    next_states = jnp.concatenate([updated[1:], ends[-1:]], axis=0)
    return (gradient, next_states)
```

```python
import jax
import jax.numpy as jnp
from jax import lax
from jax.experimental import pallas as pl
from jax.experimental.pallas import tpu as pltpu
from jax.sharding import PartitionSpec as P

NSTEP = 4
HALO = 8
BLK = 8

advect = 0.25
coriolis = 0.1
diffuse = 0.1
defect_weight = 2.0
obs_weight = 4.0
step_length = 0.1

VMEM_LIMIT = 48 * 1024 * 1024


def vmem():
    return pl.BlockSpec(memory_space=pltpu.VMEM)


def smem():
    return pl.BlockSpec(memory_space=pltpu.SMEM)


def east(x):
    return pltpu.roll(x, x.shape[1] - 1, axis=1)


def west(x):
    return pltpu.roll(x, 1, axis=1)


def below(x, after):
    first = lax.broadcasted_iota(jnp.int32, x.shape, 0) == 0
    return pltpu.roll(jnp.where(first, after, x), BLK - 1, axis=0)


def above(x, before):
    last = lax.broadcasted_iota(jnp.int32, x.shape, 0) == BLK - 1
    return pltpu.roll(jnp.where(last, before, x), 1, axis=0)


def maps_kernel(pos_ref, cells_ref, values_ref, count_ref, total_ref):
    rows, columns = count_ref.shape[1:]
    observed = cells_ref.shape[2]
    shift = columns.bit_length() - 1
    assert columns == 1 << shift
    width = 256
    base = pos_ref[0]
    row_iota = lax.broadcasted_iota(jnp.int32, (rows, observed), 0)
    col_iota = lax.broadcasted_iota(jnp.int32, (width, observed), 0)
    for step in range(NSTEP):
        cells = cells_ref[0, step : step + 1, :]
        values = obs_weight * values_ref[0, step : step + 1, :]
        row = lax.shift_right_logical(cells, shift)
        col = cells - lax.shift_left(row, shift)
        inside = row_iota == row - base
        first = values.astype(jnp.bfloat16).astype(jnp.float32)
        rest = values - first
        second = rest.astype(jnp.bfloat16).astype(jnp.float32)
        third = rest - second
        zero = jnp.zeros((rows, observed), jnp.float32)
        parts = [
            jnp.where(inside, jnp.broadcast_to(part, (rows, observed)), zero).astype(jnp.bfloat16)
            for part in (first, second, third)
        ]
        picks = jnp.where(inside, jnp.float32(obs_weight), zero).astype(jnp.bfloat16)
        left = jnp.concatenate([picks] + parts, axis=0)
        for start in range(0, columns, width):
            hot = jnp.where(col_iota == col - start, jnp.float32(1), jnp.float32(0))
            hot = hot.astype(jnp.bfloat16)
            out = lax.dot_general(
                left, hot, (((1,), (1,)), ((), ())), preferred_element_type=jnp.float32
            )
            count_ref[step, :, start : start + width] = out[:rows]
            total_ref[step, :, start : start + width] = (
                out[rows : 2 * rows] + out[2 * rows : 3 * rows] + out[3 * rows :]
            )


def forward_kernel(
    pos_ref, states_ref, up_ref, down_ref, mask_ref, path_ref, land_ref, ends_ref
):
    strip = states_ref.shape[2]
    rows = strip + 2 * HALO
    blocks = rows // BLK
    columns = states_ref.shape[3]
    base = pos_ref[0]
    grid_rows = pos_ref[1]
    path_ref[0, :, :HALO] = up_ref[:3]
    path_ref[0, :, HALO : HALO + strip] = states_ref[0]
    path_ref[0, :, HALO + strip :] = down_ref[:3]
    land_ref[:HALO] = up_ref[3]
    land_ref[HALO : HALO + strip] = mask_ref[...].astype(jnp.float32)
    land_ref[HALO + strip :] = down_ref[3]

    for step in range(NSTEP):
        for i in range(blocks):
            at = slice(i * BLK, (i + 1) * BLK)
            prior = slice(max(i - 1, 0) * BLK, (max(i - 1, 0) + 1) * BLK)
            follow = slice(min(i + 1, blocks - 1) * BLK, (min(i + 1, blocks - 1) + 1) * BLK)
            h, u, v = (path_ref[step, f, at] for f in range(3))
            h0, u0, v0 = (path_ref[step, f, prior] for f in range(3))
            h2, u2, v2 = (path_ref[step, f, follow] for f in range(3))
            hn, un, vn = below(h, h2), below(u, u2), below(v, v2)
            hs, us, vs = above(h, h0), above(u, u0), above(v, v0)
            land = land_ref[at]
            half = advect / 2.0
            dh = diffuse * h
            fx = half * ((1.0 + h) * u)
            gy = half * ((1.0 + hn) * vn - (1.0 + hs) * vs)
            keep = 1.0 - 4.0 * diffuse
            h_new = keep * h + diffuse * (hn + hs) - gy + east(dh - fx) + west(dh + fx)
            du = diffuse * u
            sx = half * h
            u_new = land * (
                keep * u + coriolis * v + diffuse * (un + us) + east(du - sx) + west(du + sx)
            )
            v_new = land * (
                keep * v
                - coriolis * u
                + diffuse * (vn + vs + east(v) + west(v))
                - half * (hn - hs)
            )
            number = base + i * BLK + lax.broadcasted_iota(jnp.int32, (BLK, columns), 0)
            inside = (number >= 0) & (number < grid_rows)
            h_new = jnp.where(inside, h_new, 0.0)
            path_ref[step + 1, 0, at] = h_new
            path_ref[step + 1, 1, at] = u_new
            path_ref[step + 1, 2, at] = v_new
    ends_ref[...] = path_ref[NSTEP, :, HALO : HALO + strip]


def adjoint_kernel(
    pos_ref, path_ref, land_ref, count_ref, total_ref, next_ref, rim_ref, out_ref, send_ref, work
):
    strip = out_ref.shape[1]
    rows = strip + 2 * HALO
    blocks = rows // BLK
    columns = out_ref.shape[2]
    base = pos_ref[0]
    grid_rows = pos_ref[1]
    weight = jnp.where(pos_ref[2] == 1, 0.0, defect_weight).astype(jnp.float32)
    half = advect / 2.0
    keep = 1.0 - 4.0 * diffuse

    def put(slot, step, i, lam):
        at = slice(i * BLK, (i + 1) * BLK)
        number = base + i * BLK + lax.broadcasted_iota(jnp.int32, (BLK, columns), 0)
        inside = (number >= 0) & (number < grid_rows)
        force = count_ref[step, at] * path_ref[step + 1, 0, at] - total_ref[step, at]
        land = land_ref[at]
        work[slot, 0, at] = jnp.where(inside, lam[0] + force, 0.0)
        work[slot, 1, at] = land * lam[1]
        work[slot, 2, at] = land * lam[2]

    for i in range(blocks):
        at = slice(i * BLK, (i + 1) * BLK)
        lam = []
        for f in range(3):
            if i == 0 or i == blocks - 1:
                ahead = rim_ref[f]
            else:
                ahead = next_ref[f, (i - 1) * BLK : i * BLK]
            lam.append(weight * (path_ref[NSTEP, f, at] - ahead))
        put(0, NSTEP - 1, i, lam)

    slot = 0
    for step in reversed(range(NSTEP)):
        inner = range(blocks) if step > 0 else range(1, blocks - 1)
        for i in inner:
            at = slice(i * BLK, (i + 1) * BLK)
            prior = slice(max(i - 1, 0) * BLK, (max(i - 1, 0) + 1) * BLK)
            follow = slice(min(i + 1, blocks - 1) * BLK, (min(i + 1, blocks - 1) + 1) * BLK)
            a, b, c = (work[slot, f, at] for f in range(3))
            a0, b0, c0 = (work[slot, f, prior] for f in range(3))
            a2, b2, c2 = (work[slot, f, follow] for f in range(3))
            an, bn, cn = below(a, a2), below(b, b2), below(c, c2)
            as_, bs, cs = above(a, a0), above(b, b0), above(c, c0)
            ae, aw = east(a), west(a)
            be, bw = east(b), west(b)
            ce, cw = east(c), west(c)
            h, u, v = (path_ref[step, f, at] for f in range(3))
            fx = half * (ae - aw)
            gy = half * (an - as_)
            depth = 1.0 + h
            lh = (
                keep * a
                + diffuse * (ae + aw + an + as_)
                + u * fx
                + v * gy
                + half * (be - bw + cn - cs)
            )
            lu = depth * fx + keep * b - coriolis * c + diffuse * (be + bw + bn + bs)
            lv = depth * gy + keep * c + coriolis * b + diffuse * (ce + cw + cn + cs)
            if step > 0:
                put(1 - slot, step - 1, i, (lh, lu, lv))
            else:
                here = slice((i - 1) * BLK, i * BLK)
                for f, (lam, x) in enumerate(((lh, h), (lu, u), (lv, v))):
                    out_ref[f, here] = lam
                    send_ref[f, here] = (
                        1.0 - step_length * defect_weight
                    ) * x - step_length * lam
        slot = 1 - slot


def shifted(block, axis, distance):
    devices = range(lax.axis_size(axis))
    route = [(i - distance, i) for i in devices if i - distance in devices]
    return lax.ppermute(block, axis, route)


def local(states, background, obs_cells, obs_values, land_mask):
    strip, columns = states.shape[2], states.shape[3]
    rows = strip + 2 * HALO
    at_first = lax.axis_index("tm") == 0
    at_final = lax.axis_index("tm") == lax.axis_size("tm") - 1
    base = lax.axis_index("space") * strip - HALO
    pos = jnp.stack(
        [base, jnp.int32(strip) * lax.axis_size("space"), at_final.astype(jnp.int32)]
    ).astype(jnp.int32)
    f32 = jnp.float32
    params = pltpu.CompilerParams(vmem_limit_bytes=VMEM_LIMIT)

    ahead = shifted(states[0], "tm", -1)
    top = jnp.concatenate([states[0, :, :HALO], land_mask[None, :HALO].astype(f32)])
    bottom = jnp.concatenate(
        [states[0, :, strip - HALO :], land_mask[None, strip - HALO :].astype(f32)]
    )
    up = shifted(bottom, "space", 1)
    down = shifted(top, "space", -1)

    half_rows = lax.broadcasted_iota(jnp.int32, (3, HALO, columns), 1) < HALO // 2
    rim = shifted(jnp.where(half_rows, down[:3], up[:3]), "tm", -1)

    count, total = pl.pallas_call(
        maps_kernel,
        out_shape=(
            jax.ShapeDtypeStruct((NSTEP, rows, columns), f32),
            jax.ShapeDtypeStruct((NSTEP, rows, columns), f32),
        ),
        in_specs=[smem(), vmem(), vmem()],
        out_specs=(vmem(), vmem()),
        compiler_params=params,
        name="maps",
    )(pos, obs_cells, obs_values)

    path, land, ends = pl.pallas_call(
        forward_kernel,
        out_shape=(
            jax.ShapeDtypeStruct((NSTEP + 1, 3, rows, columns), f32),
            jax.ShapeDtypeStruct((rows, columns), f32),
            jax.ShapeDtypeStruct((3, strip, columns), f32),
        ),
        in_specs=[smem()] + [vmem()] * 4,
        out_specs=(vmem(), vmem(), vmem()),
        compiler_params=params,
        name="forward",
    )(pos, states, up, down, land_mask)

    previous = shifted(ends, "tm", 1)

    adjoint, send = pl.pallas_call(
        adjoint_kernel,
        out_shape=(
            jax.ShapeDtypeStruct((3, strip, columns), f32),
            jax.ShapeDtypeStruct((3, strip, columns), f32),
        ),
        in_specs=[smem()] + [vmem()] * 6,
        out_specs=(vmem(), vmem()),
        scratch_shapes=[pltpu.VMEM((2, 3, rows, columns), f32)],
        compiler_params=params,
        name="adjoint",
    )(pos, path, land, count, total, ahead, rim)

    arriving = shifted(send, "tm", -1)
    previous = jnp.where(at_first, background, previous)
    gradient = defect_weight * (states[0] - previous) + adjoint
    share = jnp.where(at_final, 1.0, step_length * defect_weight).astype(f32)
    next_state = arriving + share * ends
    return (gradient[None], next_state[None])


def solution(mesh):
    in_specs = (
        P("tm", None, "space", None),
        P(None, "space", None),
        P("tm", None, None),
        P("tm", None, None),
        P("space", None),
    )
    out_specs = (P("tm", None, "space", None), P("tm", None, "space", None))
    return jax.shard_map(local, mesh=mesh, in_specs=in_specs, out_specs=out_specs, check_vma=False)
```

```python
import jax
import jax.numpy as jnp
from jax import lax
from jax.experimental import pallas as pl
from jax.experimental.pallas import tpu as pltpu
from jax.sharding import PartitionSpec as P

NSTEP = 4
HALO = 8
BLK = 8

advect = 0.25
coriolis = 0.1
diffuse = 0.1
defect_weight = 2.0
obs_weight = 4.0
step_length = 0.1


def vmem():
    return pl.BlockSpec(memory_space=pltpu.VMEM)


def smem():
    return pl.BlockSpec(memory_space=pltpu.SMEM)


def east(x):
    return pltpu.roll(x, x.shape[1] - 1, axis=1)


def west(x):
    return pltpu.roll(x, 1, axis=1)


def below(x, after):
    first = lax.broadcasted_iota(jnp.int32, x.shape, 0) == 0
    return pltpu.roll(jnp.where(first, after, x), BLK - 1, axis=0)


def above(x, before):
    last = lax.broadcasted_iota(jnp.int32, x.shape, 0) == BLK - 1
    return pltpu.roll(jnp.where(last, before, x), 1, axis=0)


def maps_kernel(pos_ref, cells_ref, values_ref, count_ref, total_ref):
    rows, columns = count_ref.shape[1:]
    observed = cells_ref.shape[2]
    shift = columns.bit_length() - 1
    assert columns == 1 << shift
    width = 256
    base = pos_ref[0]
    row_iota = lax.broadcasted_iota(jnp.int32, (rows, observed), 0)
    col_iota = lax.broadcasted_iota(jnp.int32, (width, observed), 0)
    for step in range(NSTEP):
        cells = cells_ref[0, step : step + 1, :]
        values = obs_weight * values_ref[0, step : step + 1, :]
        row = lax.shift_right_logical(cells, shift)
        col = cells - lax.shift_left(row, shift)
        inside = row_iota == row - base
        first = values.astype(jnp.bfloat16).astype(jnp.float32)
        rest = values - first
        second = rest.astype(jnp.bfloat16).astype(jnp.float32)
        third = rest - second
        zero = jnp.zeros((rows, observed), jnp.float32)
        parts = [
            jnp.where(inside, jnp.broadcast_to(part, (rows, observed)), zero).astype(jnp.bfloat16)
            for part in (first, second, third)
        ]
        picks = jnp.where(inside, jnp.float32(obs_weight), zero).astype(jnp.bfloat16)
        left = jnp.concatenate([picks] + parts, axis=0)
        for start in range(0, columns, width):
            hot = jnp.where(col_iota == col - start, jnp.float32(1), jnp.float32(0))
            hot = hot.astype(jnp.bfloat16)
            out = lax.dot_general(
                left, hot, (((1,), (1,)), ((), ())), preferred_element_type=jnp.float32
            )
            count_ref[step, :, start : start + width] = out[:rows]
            total_ref[step, :, start : start + width] = (
                out[rows : 2 * rows] + out[2 * rows : 3 * rows] + out[3 * rows :]
            )


def forward_kernel(
    pos_ref, states_ref, up_ref, down_ref, mask_ref, count_ref, land_ref, ends_ref, *path_ref
):
    strip = states_ref.shape[2]
    rows = strip + 2 * HALO
    blocks = rows // BLK
    columns = states_ref.shape[3]
    base = pos_ref[0]
    grid_rows = pos_ref[1]
    path_ref[0][:, :HALO] = up_ref[:3]
    path_ref[0][:, HALO : HALO + strip] = states_ref[0]
    path_ref[0][:, HALO + strip :] = down_ref[:3]
    land_ref[:HALO] = up_ref[3]
    land_ref[HALO : HALO + strip] = mask_ref[...].astype(jnp.float32)
    land_ref[HALO + strip :] = down_ref[3]

    for step in range(NSTEP):
        for i in range(blocks):
            at = slice(i * BLK, (i + 1) * BLK)
            prior = slice(max(i - 1, 0) * BLK, (max(i - 1, 0) + 1) * BLK)
            follow = slice(min(i + 1, blocks - 1) * BLK, (min(i + 1, blocks - 1) + 1) * BLK)
            h, u, v = (path_ref[step][f, at] for f in range(3))
            h0, u0, v0 = (path_ref[step][f, prior] for f in range(3))
            h2, u2, v2 = (path_ref[step][f, follow] for f in range(3))
            hn, un, vn = below(h, h2), below(u, u2), below(v, v2)
            hs, us, vs = above(h, h0), above(u, u0), above(v, v0)
            land = land_ref[at]
            half = advect / 2.0
            dh = diffuse * h
            fx = half * ((1.0 + h) * u)
            gy = half * ((1.0 + hn) * vn - (1.0 + hs) * vs)
            keep = 1.0 - 4.0 * diffuse
            h_new = keep * h + diffuse * (hn + hs) - gy + east(dh - fx) + west(dh + fx)
            du = diffuse * u
            sx = half * h
            u_new = land * (
                keep * u + coriolis * v + diffuse * (un + us) + east(du - sx) + west(du + sx)
            )
            v_new = land * (
                keep * v
                - coriolis * u
                + diffuse * (vn + vs + east(v) + west(v))
                - half * (hn - hs)
            )
            number = base + i * BLK + lax.broadcasted_iota(jnp.int32, (BLK, columns), 0)
            inside = (number >= 0) & (number < grid_rows)
            h_new = jnp.where(inside, h_new, 0.0)
            path_ref[step + 1][0, at] = h_new
            path_ref[step + 1][1, at] = u_new
            path_ref[step + 1][2, at] = v_new
    ends_ref[...] = path_ref[NSTEP][:, HALO : HALO + strip]


def adjoint_kernel(part):
    def kernel(*refs):
        if part == "middle":
            pos_ref, land_ref, count_ref, total_ref, *path_ref = refs[: NSTEP + 5]
            next_ref, out_ref, send_ref, work = refs[NSTEP + 5 :]
        else:
            pos_ref, land_ref, count_ref, total_ref, *path_ref = refs[: NSTEP + 5]
            rim_ref, work_ref, out_ref, send_ref, work = refs[NSTEP + 5 :]
        rows, columns = land_ref.shape
        blocks = rows // BLK
        base = pos_ref[0]
        grid_rows = pos_ref[1]
        weight = jnp.where(pos_ref[2] == 1, 0.0, defect_weight).astype(jnp.float32)
        half = advect / 2.0
        keep = 1.0 - 4.0 * diffuse
        edge = (0, 1, blocks - 2, blocks - 1)
        if part == "middle":
            first = range(1, blocks - 1)
            inner = range(1, blocks - 1)
            final = range(2, blocks - 2)
        else:
            first = (0, blocks - 1)
            inner = edge
            final = (1, blocks - 2)

        def get(step, f, i):
            at = slice(i * BLK, (i + 1) * BLK)
            if part == "edge" and (i not in edge or (step == NSTEP - 1 and i in (1, blocks - 2))):
                return work_ref[step, f, at]
            return work[step, f, at]

        def put(step, i, lam):
            at = slice(i * BLK, (i + 1) * BLK)
            number = base + i * BLK + lax.broadcasted_iota(jnp.int32, (BLK, columns), 0)
            inside = (number >= 0) & (number < grid_rows)
            force = count_ref[step, at] * path_ref[step + 1][0, at] - total_ref[step, at]
            land = land_ref[at]
            work[step, 0, at] = jnp.where(inside, lam[0] + force, 0.0)
            work[step, 1, at] = land * lam[1]
            work[step, 2, at] = land * lam[2]

        for i in first:
            at = slice(i * BLK, (i + 1) * BLK)
            if part == "middle":
                ahead = [next_ref[f, (i - 1) * BLK : i * BLK] for f in range(3)]
            else:
                ahead = [rim_ref[f] for f in range(3)]
            put(
                NSTEP - 1,
                i,
                [weight * (path_ref[NSTEP][f, at] - ahead[f]) for f in range(3)],
            )

        for step in reversed(range(NSTEP)):
            for n, i in enumerate(inner if step > 0 else final):
                at = slice(i * BLK, (i + 1) * BLK)
                before, after = max(i - 1, first[0]), min(i + 1, first[-1])
                a, b, c = (get(step, f, i) for f in range(3))
                a0, b0, c0 = (get(step, f, before) for f in range(3))
                a2, b2, c2 = (get(step, f, after) for f in range(3))
                an, bn, cn = below(a, a2), below(b, b2), below(c, c2)
                as_, bs, cs = above(a, a0), above(b, b0), above(c, c0)
                ae, aw = east(a), west(a)
                be, bw = east(b), west(b)
                ce, cw = east(c), west(c)
                h, u, v = (path_ref[step][f, at] for f in range(3))
                fx = half * (ae - aw)
                gy = half * (an - as_)
                depth = 1.0 + h
                lh = (
                    keep * a
                    + diffuse * (ae + aw + an + as_)
                    + u * fx
                    + v * gy
                    + half * (be - bw + cn - cs)
                )
                lu = depth * fx + keep * b - coriolis * c + diffuse * (be + bw + bn + bs)
                lv = depth * gy + keep * c + coriolis * b + diffuse * (ce + cw + cn + cs)
                if step > 0:
                    put(step - 1, i, (lh, lu, lv))
                else:
                    here = slice(n * BLK, (n + 1) * BLK)
                    for f, (lam, x) in enumerate(((lh, h), (lu, u), (lv, v))):
                        out_ref[f, here] = lam
                        send_ref[f, here] = (
                            1.0 - step_length * defect_weight
                        ) * x - step_length * lam

    return kernel


def shifted(block, axis, distance):
    devices = range(lax.axis_size(axis))
    route = [(i - distance, i) for i in devices if i - distance in devices]
    return lax.ppermute(block, axis, route)


def local(states, background, obs_cells, obs_values, land_mask):
    strip, columns = states.shape[2], states.shape[3]
    rows = strip + 2 * HALO
    at_first = lax.axis_index("tm") == 0
    at_final = lax.axis_index("tm") == lax.axis_size("tm") - 1
    base = lax.axis_index("space") * strip - HALO
    pos = jnp.stack(
        [base, jnp.int32(strip) * lax.axis_size("space"), at_final.astype(jnp.int32)]
    ).astype(jnp.int32)
    f32 = jnp.float32

    def params(megabytes):
        return pltpu.CompilerParams(vmem_limit_bytes=megabytes * 1024 * 1024)

    def cost(us):
        return pl.CostEstimate(
            flops=1000, transcendentals=0, bytes_accessed=int(us * 3.0e6)
        )

    top = jnp.concatenate([states[0, :, :HALO], land_mask[None, :HALO].astype(f32)])
    bottom = jnp.concatenate(
        [states[0, :, strip - HALO :], land_mask[None, strip - HALO :].astype(f32)]
    )
    share = jnp.where(at_final, 1.0, step_length * defect_weight).astype(f32)
    top, bottom, moving, pos, at_first, share = lax.optimization_barrier(
        (top, bottom, states[0], pos, at_first, share)
    )
    up = shifted(bottom, "space", 1)
    down = shifted(top, "space", -1)
    ahead = shifted(moving, "tm", -1)

    count, total = pl.pallas_call(
        maps_kernel,
        out_shape=(
            jax.ShapeDtypeStruct((NSTEP, rows, columns), f32),
            jax.ShapeDtypeStruct((NSTEP, rows, columns), f32),
        ),
        in_specs=[smem(), vmem(), vmem()],
        out_specs=(vmem(), vmem()),
        compiler_params=params(16),
        cost_estimate=cost(3.5),
        name="maps",
    )(pos, obs_cells, obs_values)

    half_rows = lax.broadcasted_iota(jnp.int32, (3, HALO, columns), 1) < HALO // 2
    rim = jnp.where(half_rows, down[:3], up[:3])
    rim, up, down = lax.optimization_barrier((rim, up, down))
    rim = shifted(rim, "tm", -1)

    land, ends, *path = pl.pallas_call(
        forward_kernel,
        out_shape=(
            jax.ShapeDtypeStruct((rows, columns), f32),
            jax.ShapeDtypeStruct((3, strip, columns), f32),
        )
        + (jax.ShapeDtypeStruct((3, rows, columns), f32),) * (NSTEP + 1),
        in_specs=[smem()] + [vmem()] * 4 + [pl.BlockSpec(memory_space=pl.ANY)],
        out_specs=(vmem(),) * (NSTEP + 3),
        compiler_params=params(16),
        cost_estimate=cost(5),
        name="forward",
    )(pos, states, up, down, land_mask, count)

    previous = shifted(ends, "tm", 1)

    def adjoint(part, height, *operands):
        shapes = [jax.ShapeDtypeStruct((3, height, columns), f32)] * 2
        scratch = [pltpu.VMEM((NSTEP, 3, rows, columns), f32)]
        if part == "middle":
            shapes.append(jax.ShapeDtypeStruct((NSTEP, 3, rows, columns), f32))
            scratch = []
        return pl.pallas_call(
            adjoint_kernel(part),
            out_shape=tuple(shapes),
            in_specs=[smem()] + [vmem()] * len(operands),
            out_specs=(vmem(),) * len(shapes),
            scratch_shapes=scratch,
            compiler_params=params(24),
            cost_estimate=cost(4 if part == "middle" else 2),
            name="adjoint_" + part,
        )(pos, *operands)

    shared = (land, count, total, *path)
    mid_adj, mid_send, work = adjoint("middle", strip - 2 * BLK, *shared, ahead)
    mid_next = shifted(mid_send, "tm", -1)
    edge_adj, edge_send = adjoint("edge", 2 * BLK, *shared, rim, work)
    edge_next = shifted(edge_send, "tm", -1)

    def joined(middle, edge):
        return jnp.concatenate([edge[:, :BLK], middle, edge[:, BLK:]], axis=1)

    previous = jnp.where(at_first, background, previous)
    gradient = defect_weight * (states[0] - previous) + joined(mid_adj, edge_adj)
    next_state = joined(mid_next, edge_next) + share * ends
    return (gradient[None], next_state[None])


def solution(mesh):
    in_specs = (
        P("tm", None, "space", None),
        P(None, "space", None),
        P("tm", None, None),
        P("tm", None, None),
        P("space", None),
    )
    out_specs = (P("tm", None, "space", None), P("tm", None, "space", None))
    return jax.shard_map(local, mesh=mesh, in_specs=in_specs, out_specs=out_specs, check_vma=False)
```

```python
import jax
import jax.numpy as jnp
from jax import lax
from jax.experimental import pallas as pl
from jax.experimental.pallas import tpu as pltpu
from jax.sharding import PartitionSpec as P

NSTEP = 4
HALO = 8
BLK = 8

advect = 0.25
coriolis = 0.1
diffuse = 0.1
defect_weight = 2.0
obs_weight = 4.0
step_length = 0.1


def vmem():
    return pl.BlockSpec(memory_space=pltpu.VMEM)


def smem():
    return pl.BlockSpec(memory_space=pltpu.SMEM)


def east(x):
    return pltpu.roll(x, x.shape[1] - 1, axis=1)


def west(x):
    return pltpu.roll(x, 1, axis=1)


def below(x, after):
    first = lax.broadcasted_iota(jnp.int32, x.shape, 0) == 0
    return pltpu.roll(jnp.where(first, after, x), BLK - 1, axis=0)


def above(x, before):
    last = lax.broadcasted_iota(jnp.int32, x.shape, 0) == BLK - 1
    return pltpu.roll(jnp.where(last, before, x), 1, axis=0)


def maps_kernel(pos_ref, cells_ref, values_ref, count_ref, total_ref):
    rows, columns = count_ref.shape[1:]
    observed = cells_ref.shape[2]
    shift = columns.bit_length() - 1
    assert columns == 1 << shift
    width = 256
    base = pos_ref[0]
    row_iota = lax.broadcasted_iota(jnp.int32, (rows, observed), 0)
    col_iota = lax.broadcasted_iota(jnp.int32, (width, observed), 0)
    for step in range(NSTEP):
        cells = cells_ref[0, step : step + 1, :]
        values = obs_weight * values_ref[0, step : step + 1, :]
        row = lax.shift_right_logical(cells, shift)
        col = cells - lax.shift_left(row, shift)
        inside = row_iota == row - base
        first = values.astype(jnp.bfloat16).astype(jnp.float32)
        rest = values - first
        second = rest.astype(jnp.bfloat16).astype(jnp.float32)
        third = rest - second
        zero = jnp.zeros((rows, observed), jnp.float32)
        parts = [
            jnp.where(inside, jnp.broadcast_to(part, (rows, observed)), zero).astype(jnp.bfloat16)
            for part in (first, second, third)
        ]
        picks = jnp.where(inside, jnp.float32(obs_weight), zero).astype(jnp.bfloat16)
        left = jnp.concatenate([picks] + parts, axis=0)
        for start in range(0, columns, width):
            hot = jnp.where(col_iota == col - start, jnp.float32(1), jnp.float32(0))
            hot = hot.astype(jnp.bfloat16)
            out = lax.dot_general(
                left, hot, (((1,), (1,)), ((), ())), preferred_element_type=jnp.float32
            )
            count_ref[step, :, start : start + width] = out[:rows]
            total_ref[step, :, start : start + width] = (
                out[rows : 2 * rows] + out[2 * rows : 3 * rows] + out[3 * rows :]
            )


def forward_kernel(
    pos_ref, states_ref, up_ref, down_ref, mask_ref, count_ref, land_ref, ends_ref, *path_ref
):
    strip = states_ref.shape[2]
    rows = strip + 2 * HALO
    blocks = rows // BLK
    columns = states_ref.shape[3]
    base = pos_ref[0]
    grid_rows = pos_ref[1]
    path_ref[0][:, :HALO] = up_ref[:3]
    path_ref[0][:, HALO : HALO + strip] = states_ref[0]
    path_ref[0][:, HALO + strip :] = down_ref[:3]
    land_ref[:HALO] = up_ref[3]
    land_ref[HALO : HALO + strip] = mask_ref[...].astype(jnp.float32)
    land_ref[HALO + strip :] = down_ref[3]

    for step in range(NSTEP):
        for i in range(blocks):
            at = slice(i * BLK, (i + 1) * BLK)
            prior = slice(max(i - 1, 0) * BLK, (max(i - 1, 0) + 1) * BLK)
            follow = slice(min(i + 1, blocks - 1) * BLK, (min(i + 1, blocks - 1) + 1) * BLK)
            h, u, v = (path_ref[step][f, at] for f in range(3))
            h0, u0, v0 = (path_ref[step][f, prior] for f in range(3))
            h2, u2, v2 = (path_ref[step][f, follow] for f in range(3))
            hn, un, vn = below(h, h2), below(u, u2), below(v, v2)
            hs, us, vs = above(h, h0), above(u, u0), above(v, v0)
            land = land_ref[at]
            half = advect / 2.0
            dh = diffuse * h
            fx = half * ((1.0 + h) * u)
            gy = half * ((1.0 + hn) * vn - (1.0 + hs) * vs)
            keep = 1.0 - 4.0 * diffuse
            h_new = keep * h + diffuse * (hn + hs) - gy + east(dh - fx) + west(dh + fx)
            du = diffuse * u
            sx = half * h
            u_new = land * (
                keep * u + coriolis * v + diffuse * (un + us) + east(du - sx) + west(du + sx)
            )
            v_new = land * (
                keep * v
                - coriolis * u
                + diffuse * (vn + vs + east(v) + west(v))
                - half * (hn - hs)
            )
            number = base + i * BLK + lax.broadcasted_iota(jnp.int32, (BLK, columns), 0)
            inside = (number >= 0) & (number < grid_rows)
            h_new = jnp.where(inside, h_new, 0.0)
            path_ref[step + 1][0, at] = h_new
            path_ref[step + 1][1, at] = u_new
            path_ref[step + 1][2, at] = v_new
    ends_ref[...] = path_ref[NSTEP][:, HALO : HALO + strip]


def adjoint_kernel(part):
    def kernel(*refs):
        if part == "middle":
            pos_ref, land_ref, count_ref, total_ref, *path_ref = refs[: NSTEP + 5]
            next_ref, out_ref, send_ref, work = refs[NSTEP + 5 :]
        else:
            pos_ref, land_ref, count_ref, total_ref, *path_ref = refs[: NSTEP + 5]
            rim_ref, work_ref, out_ref, send_ref, work = refs[NSTEP + 5 :]
        rows, columns = land_ref.shape
        blocks = rows // BLK
        base = pos_ref[0]
        grid_rows = pos_ref[1]
        weight = jnp.where(pos_ref[2] == 1, 0.0, defect_weight).astype(jnp.float32)
        half = advect / 2.0
        keep = 1.0 - 4.0 * diffuse
        edge = (0, 1, blocks - 2, blocks - 1)
        if part == "middle":
            first = range(1, blocks - 1)
            inner = range(1, blocks - 1)
            final = range(2, blocks - 2)
        else:
            first = (0, blocks - 1)
            inner = edge
            final = (1, blocks - 2)

        def get(step, f, i):
            at = slice(i * BLK, (i + 1) * BLK)
            if part == "edge" and (i not in edge or (step == NSTEP - 1 and i in (1, blocks - 2))):
                return work_ref[step, f, at]
            return work[step, f, at]

        def put(step, i, lam):
            at = slice(i * BLK, (i + 1) * BLK)
            number = base + i * BLK + lax.broadcasted_iota(jnp.int32, (BLK, columns), 0)
            inside = (number >= 0) & (number < grid_rows)
            force = count_ref[step, at] * path_ref[step + 1][0, at] - total_ref[step, at]
            land = land_ref[at]
            work[step, 0, at] = jnp.where(inside, lam[0] + force, 0.0)
            work[step, 1, at] = land * lam[1]
            work[step, 2, at] = land * lam[2]

        for i in first:
            at = slice(i * BLK, (i + 1) * BLK)
            if part == "middle":
                ahead = [next_ref[f, (i - 1) * BLK : i * BLK] for f in range(3)]
            else:
                ahead = [rim_ref[f] for f in range(3)]
            put(
                NSTEP - 1,
                i,
                [weight * (path_ref[NSTEP][f, at] - ahead[f]) for f in range(3)],
            )

        for step in reversed(range(NSTEP)):
            for n, i in enumerate(inner if step > 0 else final):
                at = slice(i * BLK, (i + 1) * BLK)
                before, after = max(i - 1, first[0]), min(i + 1, first[-1])
                a, b, c = (get(step, f, i) for f in range(3))
                a0, b0, c0 = (get(step, f, before) for f in range(3))
                a2, b2, c2 = (get(step, f, after) for f in range(3))
                an, bn, cn = below(a, a2), below(b, b2), below(c, c2)
                as_, bs, cs = above(a, a0), above(b, b0), above(c, c0)
                ae, aw = east(a), west(a)
                be, bw = east(b), west(b)
                ce, cw = east(c), west(c)
                h, u, v = (path_ref[step][f, at] for f in range(3))
                fx = half * (ae - aw)
                gy = half * (an - as_)
                depth = 1.0 + h
                lh = (
                    keep * a
                    + diffuse * (ae + aw + an + as_)
                    + u * fx
                    + v * gy
                    + half * (be - bw + cn - cs)
                )
                lu = depth * fx + keep * b - coriolis * c + diffuse * (be + bw + bn + bs)
                lv = depth * gy + keep * c + coriolis * b + diffuse * (ce + cw + cn + cs)
                if step > 0:
                    put(step - 1, i, (lh, lu, lv))
                else:
                    here = slice(n * BLK, (n + 1) * BLK)
                    for f, (lam, x) in enumerate(((lh, h), (lu, u), (lv, v))):
                        out_ref[f, here] = lam
                        send_ref[f, here] = (
                            1.0 - step_length * defect_weight
                        ) * x - step_length * lam

    return kernel


def shifted(block, axis, distance):
    devices = range(lax.axis_size(axis))
    route = [(i - distance, i) for i in devices if i - distance in devices]
    return lax.ppermute(block, axis, route)


def local(states, background, obs_cells, obs_values, land_mask):
    strip, columns = states.shape[2], states.shape[3]
    rows = strip + 2 * HALO
    at_first = lax.axis_index("tm") == 0
    at_final = lax.axis_index("tm") == lax.axis_size("tm") - 1
    base = lax.axis_index("space") * strip - HALO
    pos = jnp.stack(
        [base, jnp.int32(strip) * lax.axis_size("space"), at_final.astype(jnp.int32)]
    ).astype(jnp.int32)
    f32 = jnp.float32

    def params(megabytes):
        return pltpu.CompilerParams(vmem_limit_bytes=megabytes * 1024 * 1024)

    def cost(us):
        return pl.CostEstimate(
            flops=int(us * 1.0e9), transcendentals=0, bytes_accessed=int(us * 3.0e6)
        )

    share = jnp.where(at_final, 1.0, step_length * defect_weight).astype(f32)
    parts = (
        states[0, :, :HALO],
        states[0, :, strip - HALO :],
        land_mask[None, :HALO].astype(f32),
        land_mask[None, strip - HALO :].astype(f32),
    )
    parts, moving, pos, at_first, share = lax.optimization_barrier(
        (parts, states[0], pos, at_first, share)
    )
    ahead = shifted(moving, "tm", -1)
    up = shifted(jnp.concatenate([parts[1], parts[3]]), "space", 1)
    down = shifted(jnp.concatenate([parts[0], parts[2]]), "space", -1)

    count, total = pl.pallas_call(
        maps_kernel,
        out_shape=(
            jax.ShapeDtypeStruct((NSTEP, rows, columns), f32),
            jax.ShapeDtypeStruct((NSTEP, rows, columns), f32),
        ),
        in_specs=[smem(), vmem(), vmem()],
        out_specs=(vmem(), vmem()),
        compiler_params=params(16),
        cost_estimate=cost(1),
        name="maps",
    )(pos, obs_cells, obs_values)

    half_rows = lax.broadcasted_iota(jnp.int32, (3, HALO, columns), 1) < HALO // 2
    rim = jnp.where(half_rows, down[:3], up[:3])
    rim, up, down = lax.optimization_barrier((rim, up, down))
    rim = shifted(rim, "tm", -1)

    land, ends, *path = pl.pallas_call(
        forward_kernel,
        out_shape=(
            jax.ShapeDtypeStruct((rows, columns), f32),
            jax.ShapeDtypeStruct((3, strip, columns), f32),
        )
        + (jax.ShapeDtypeStruct((3, rows, columns), f32),) * (NSTEP + 1),
        in_specs=[smem()] + [vmem()] * 4 + [pl.BlockSpec(memory_space=pl.ANY)],
        out_specs=(vmem(),) * (NSTEP + 3),
        compiler_params=params(16),
        cost_estimate=cost(2),
        name="forward",
    )(pos, states, up, down, land_mask, count)

    previous = shifted(ends, "tm", 1)

    def adjoint(part, height, *operands):
        shapes = [jax.ShapeDtypeStruct((3, height, columns), f32)] * 2
        scratch = [pltpu.VMEM((NSTEP, 3, rows, columns), f32)]
        if part == "middle":
            shapes.append(jax.ShapeDtypeStruct((NSTEP, 3, rows, columns), f32))
            scratch = []
        return pl.pallas_call(
            adjoint_kernel(part),
            out_shape=tuple(shapes),
            in_specs=[smem()] + [vmem()] * len(operands),
            out_specs=(vmem(),) * len(shapes),
            scratch_shapes=scratch,
            compiler_params=params(24),
            cost_estimate=cost(0.1 if part == "middle" else 60),
            name="adjoint_" + part,
        )(pos, *operands)

    shared = (land, count, total, *path)
    mid_adj, mid_send, work = adjoint("middle", strip - 2 * BLK, *shared, ahead)
    mid_next = shifted(mid_send, "tm", -1)
    edge_adj, edge_send = adjoint("edge", 2 * BLK, *shared, rim, work)
    edge_next = shifted(edge_send, "tm", -1)

    def joined(middle, edge):
        return jnp.concatenate([edge[:, :BLK], middle, edge[:, BLK:]], axis=1)

    previous = jnp.where(at_first, background, previous)
    gradient = defect_weight * (states[0] - previous) + joined(mid_adj, edge_adj)
    next_state = joined(mid_next, edge_next) + share * ends
    return (gradient[None], next_state[None])


def solution(mesh):
    in_specs = (
        P("tm", None, "space", None),
        P(None, "space", None),
        P("tm", None, None),
        P("tm", None, None),
        P("space", None),
    )
    out_specs = (P("tm", None, "space", None), P("tm", None, "space", None))
    return jax.shard_map(local, mesh=mesh, in_specs=in_specs, out_specs=out_specs, check_vma=False)
```

```python
import jax
import jax.numpy as jnp
from jax import lax
from jax.experimental import pallas as pl
from jax.experimental.pallas import tpu as pltpu
from jax.sharding import PartitionSpec as P

NSTEP = 4
HALO = 8
BLK = 8

advect = 0.25
coriolis = 0.1
diffuse = 0.1
defect_weight = 2.0
obs_weight = 4.0
step_length = 0.1


def vmem():
    return pl.BlockSpec(memory_space=pltpu.VMEM)


def hbm():
    return pl.BlockSpec(memory_space=pltpu.HBM)


def off_chip(x):
    return pltpu.with_memory_space_constraint(x, pltpu.HBM)


def smem():
    return pl.BlockSpec(memory_space=pltpu.SMEM)


def east(x):
    return pltpu.roll(x, x.shape[1] - 1, axis=1)


def west(x):
    return pltpu.roll(x, 1, axis=1)


def below(x, after):
    first = lax.broadcasted_iota(jnp.int32, x.shape, 0) == 0
    return pltpu.roll(jnp.where(first, after, x), BLK - 1, axis=0)


def above(x, before):
    last = lax.broadcasted_iota(jnp.int32, x.shape, 0) == BLK - 1
    return pltpu.roll(jnp.where(last, before, x), 1, axis=0)


def prepare_kernel(
    pos_ref, states_ref, mask_ref, cells_ref, values_ref,
    cross_ref, pair_ref, seen_ref, wanted_ref, bits, sems
):
    strip = states_ref.shape[2]
    bottom = strip - HALO
    odd = pos_ref[3]
    copies = []
    for n, (out, at) in enumerate(((cross_ref, odd * bottom), (pair_ref, (1 - odd) * bottom))):
        at = pl.multiple_of(at, HALO)
        copies.append(
            pltpu.make_async_copy(mask_ref.at[pl.ds(at, HALO)], bits.at[n], sems.at[2 * n])
        )
        copies.append(
            pltpu.make_async_copy(
                states_ref.at[0, :, pl.ds(at, HALO)], out.at[pl.ds(0, 3)], sems.at[2 * n + 1]
            )
        )
    copies.append(pltpu.make_async_copy(cells_ref.at[0], seen_ref, sems.at[4]))
    copies.append(pltpu.make_async_copy(values_ref.at[0], wanted_ref, sems.at[5]))
    for copy in copies:
        copy.start()
    for copy in copies:
        copy.wait()
    cross_ref[3] = bits[0].astype(jnp.float32)
    pair_ref[3] = bits[1].astype(jnp.float32)


def maps_kernel(
    pos_ref, cells_ref, values_ref, states_ref, mask_ref,
    count_ref, total_ref, start_ref, bits_ref, sems
):
    strip = mask_ref.shape[0]
    copies = (
        pltpu.make_async_copy(
            states_ref.at[0], start_ref.at[:, pl.ds(HALO, strip)], sems.at[0]
        ),
        pltpu.make_async_copy(mask_ref, bits_ref, sems.at[1]),
    )
    for copy in copies:
        copy.start()
    rows, columns = count_ref.shape[1:]
    observed = cells_ref.shape[1]
    shift = columns.bit_length() - 1
    assert columns == 1 << shift
    width = 256
    base = pos_ref[0]
    row_iota = lax.broadcasted_iota(jnp.int32, (rows, observed), 0)
    col_iota = lax.broadcasted_iota(jnp.int32, (width, observed), 0)
    for step in range(NSTEP):
        cells = cells_ref[step : step + 1, :]
        values = obs_weight * values_ref[step : step + 1, :]
        row = lax.shift_right_logical(cells, shift)
        col = cells - lax.shift_left(row, shift)
        inside = row_iota == row - base
        first = values.astype(jnp.bfloat16).astype(jnp.float32)
        rest = values - first
        second = rest.astype(jnp.bfloat16).astype(jnp.float32)
        third = rest - second
        zero = jnp.zeros((rows, observed), jnp.float32)
        parts = [
            jnp.where(inside, jnp.broadcast_to(part, (rows, observed)), zero).astype(jnp.bfloat16)
            for part in (first, second, third)
        ]
        picks = jnp.where(inside, jnp.float32(obs_weight), zero).astype(jnp.bfloat16)
        left = jnp.concatenate([picks] + parts, axis=0)
        for start in range(0, columns, width):
            hot = jnp.where(col_iota == col - start, jnp.float32(1), jnp.float32(0))
            hot = hot.astype(jnp.bfloat16)
            out = lax.dot_general(
                left, hot, (((1,), (1,)), ((), ())), preferred_element_type=jnp.float32
            )
            count_ref[step, :, start : start + width] = out[:rows]
            total_ref[step, :, start : start + width] = (
                out[rows : 2 * rows] + out[2 * rows : 3 * rows] + out[3 * rows :]
            )
    for copy in copies:
        copy.wait()


def forward_kernel(
    pos_ref, start_ref, cross_ref, pair_ref, mask_ref, land_ref, ends_ref, *path_ref
):
    strip, columns = mask_ref.shape
    rows = strip + 2 * HALO
    blocks = rows // BLK
    base = pos_ref[0]
    grid_rows = pos_ref[1]
    odd = pos_ref[3] == 1
    up = jnp.where(odd, pair_ref[...], cross_ref[...])
    down = jnp.where(odd, cross_ref[...], pair_ref[...])
    path_ref[0][:, :HALO] = up[:3]
    path_ref[0][:, HALO + strip :] = down[:3]
    land_ref[:HALO] = up[3]
    land_ref[HALO : HALO + strip] = mask_ref[...].astype(jnp.float32)
    land_ref[HALO + strip :] = down[3]

    for step in range(NSTEP):
        for i in range(blocks):
            at = slice(i * BLK, (i + 1) * BLK)
            prior = slice(max(i - 1, 0) * BLK, (max(i - 1, 0) + 1) * BLK)
            follow = slice(min(i + 1, blocks - 1) * BLK, (min(i + 1, blocks - 1) + 1) * BLK)
            h, u, v = (path_ref[step][f, at] for f in range(3))
            h0, u0, v0 = (path_ref[step][f, prior] for f in range(3))
            h2, u2, v2 = (path_ref[step][f, follow] for f in range(3))
            hn, un, vn = below(h, h2), below(u, u2), below(v, v2)
            hs, us, vs = above(h, h0), above(u, u0), above(v, v0)
            land = land_ref[at]
            half = advect / 2.0
            dh = diffuse * h
            fx = half * ((1.0 + h) * u)
            gy = half * ((1.0 + hn) * vn - (1.0 + hs) * vs)
            keep = 1.0 - 4.0 * diffuse
            h_new = keep * h + diffuse * (hn + hs) - gy + east(dh - fx) + west(dh + fx)
            du = diffuse * u
            sx = half * h
            u_new = land * (
                keep * u + coriolis * v + diffuse * (un + us) + east(du - sx) + west(du + sx)
            )
            v_new = land * (
                keep * v
                - coriolis * u
                + diffuse * (vn + vs + east(v) + west(v))
                - half * (hn - hs)
            )
            number = base + i * BLK + lax.broadcasted_iota(jnp.int32, (BLK, columns), 0)
            inside = (number >= 0) & (number < grid_rows)
            h_new = jnp.where(inside, h_new, 0.0)
            path_ref[step + 1][0, at] = h_new
            path_ref[step + 1][1, at] = u_new
            path_ref[step + 1][2, at] = v_new
    ends_ref[...] = path_ref[NSTEP][:, HALO : HALO + strip]


def adjoint_kernel(part):
    def kernel(*refs):
        if part == "middle":
            pos_ref, land_ref, count_ref, total_ref, *path_ref = refs[: NSTEP + 5]
            next_ref, out_ref, send_ref, work = refs[NSTEP + 5 :]
        else:
            pos_ref, land_ref, count_ref, total_ref, *path_ref = refs[: NSTEP + 5]
            rim_ref, work_ref, out_ref, send_ref, work = refs[NSTEP + 5 :]
        rows, columns = land_ref.shape
        blocks = rows // BLK
        base = pos_ref[0]
        grid_rows = pos_ref[1]
        weight = jnp.where(pos_ref[2] == 1, 0.0, defect_weight).astype(jnp.float32)
        half = advect / 2.0
        keep = 1.0 - 4.0 * diffuse
        edge = (0, 1, blocks - 2, blocks - 1)
        if part == "middle":
            first = range(1, blocks - 1)
            inner = range(1, blocks - 1)
            final = range(2, blocks - 2)
        else:
            first = (0, blocks - 1)
            inner = edge
            final = (1, blocks - 2)

        def get(step, f, i):
            at = slice(i * BLK, (i + 1) * BLK)
            if part == "edge" and (i not in edge or (step == NSTEP - 1 and i in (1, blocks - 2))):
                return work_ref[step, f, at]
            return work[step, f, at]

        def put(step, i, lam):
            at = slice(i * BLK, (i + 1) * BLK)
            number = base + i * BLK + lax.broadcasted_iota(jnp.int32, (BLK, columns), 0)
            inside = (number >= 0) & (number < grid_rows)
            force = count_ref[step, at] * path_ref[step + 1][0, at] - total_ref[step, at]
            land = land_ref[at]
            work[step, 0, at] = jnp.where(inside, lam[0] + force, 0.0)
            work[step, 1, at] = land * lam[1]
            work[step, 2, at] = land * lam[2]

        for i in first:
            at = slice(i * BLK, (i + 1) * BLK)
            if part == "middle":
                ahead = [next_ref[f, (i - 1) * BLK : i * BLK] for f in range(3)]
            else:
                ahead = [rim_ref[f] for f in range(3)]
            put(
                NSTEP - 1,
                i,
                [weight * (path_ref[NSTEP][f, at] - ahead[f]) for f in range(3)],
            )

        for step in reversed(range(NSTEP)):
            for n, i in enumerate(inner if step > 0 else final):
                at = slice(i * BLK, (i + 1) * BLK)
                before, after = max(i - 1, first[0]), min(i + 1, first[-1])
                a, b, c = (get(step, f, i) for f in range(3))
                a0, b0, c0 = (get(step, f, before) for f in range(3))
                a2, b2, c2 = (get(step, f, after) for f in range(3))
                an, bn, cn = below(a, a2), below(b, b2), below(c, c2)
                as_, bs, cs = above(a, a0), above(b, b0), above(c, c0)
                ae, aw = east(a), west(a)
                be, bw = east(b), west(b)
                ce, cw = east(c), west(c)
                h, u, v = (path_ref[step][f, at] for f in range(3))
                fx = half * (ae - aw)
                gy = half * (an - as_)
                depth = 1.0 + h
                lh = (
                    keep * a
                    + diffuse * (ae + aw + an + as_)
                    + u * fx
                    + v * gy
                    + half * (be - bw + cn - cs)
                )
                lu = depth * fx + keep * b - coriolis * c + diffuse * (be + bw + bn + bs)
                lv = depth * gy + keep * c + coriolis * b + diffuse * (ce + cw + cn + cs)
                if step > 0:
                    put(step - 1, i, (lh, lu, lv))
                else:
                    here = slice(n * BLK, (n + 1) * BLK)
                    for f, (lam, x) in enumerate(((lh, h), (lu, u), (lv, v))):
                        out_ref[f, here] = lam
                        send_ref[f, here] = (
                            1.0 - step_length * defect_weight
                        ) * x - step_length * lam

    return kernel


def shifted(block, axis, distance):
    devices = range(lax.axis_size(axis))
    route = [(i - distance, i) for i in devices if i - distance in devices]
    return lax.ppermute(block, axis, route)


def local(states, background, obs_cells, obs_values, land_mask):
    strip, columns = states.shape[2], states.shape[3]
    rows = strip + 2 * HALO
    at_first = lax.axis_index("tm") == 0
    at_final = lax.axis_index("tm") == lax.axis_size("tm") - 1
    base = lax.axis_index("space") * strip - HALO
    odd = lax.axis_index("space") & 1
    pos = jnp.stack(
        [base, jnp.int32(strip) * lax.axis_size("space"), at_final.astype(jnp.int32), odd]
    ).astype(jnp.int32)
    f32 = jnp.float32

    def params(megabytes):
        return pltpu.CompilerParams(vmem_limit_bytes=megabytes * 1024 * 1024)

    def cost(us):
        return pl.CostEstimate(
            flops=int(us * 1.0e9), transcendentals=0, bytes_accessed=int(us * 3.0e6)
        )

    observed = obs_cells.shape[2]
    cross, pair, cells, values = pl.pallas_call(
        prepare_kernel,
        out_shape=(
            jax.ShapeDtypeStruct((4, HALO, columns), f32),
            jax.ShapeDtypeStruct((4, HALO, columns), f32),
            jax.ShapeDtypeStruct((NSTEP, observed), jnp.int32),
            jax.ShapeDtypeStruct((NSTEP, observed), f32),
        ),
        in_specs=[smem()] + [hbm()] * 4,
        out_specs=(vmem(),) * 4,
        scratch_shapes=[
            pltpu.VMEM((2, HALO, columns), jnp.int32),
            pltpu.SemaphoreType.DMA((6,)),
        ],
        compiler_params=params(8),
        cost_estimate=cost(0.5),
        name="prepare",
    )(pos, *(off_chip(x) for x in (states, land_mask, obs_cells, obs_values)))
    share = jnp.where(at_final, 1.0, step_length * defect_weight).astype(f32)
    cross, pair, moving, pos, at_first, share, even = lax.optimization_barrier(
        (cross, pair, states[0], pos, at_first, share, odd == 0)
    )
    strips = lax.axis_size("space")
    inner = [(i, i ^ 1) for i in range(strips)]
    outer = [(i, j) for i in range(strips) for j in [((i + 1) ^ 1) - 1] if 0 <= j < strips]
    cross = lax.ppermute(cross, "space", outer)
    ahead = shifted(moving, "tm", -1)
    pair = lax.ppermute(pair, "space", inner)

    count, total, start, bits = pl.pallas_call(
        maps_kernel,
        out_shape=(
            jax.ShapeDtypeStruct((NSTEP, rows, columns), f32),
            jax.ShapeDtypeStruct((NSTEP, rows, columns), f32),
            jax.ShapeDtypeStruct((3, rows, columns), f32),
            jax.ShapeDtypeStruct((strip, columns), jnp.int32),
        ),
        in_specs=[smem(), vmem(), vmem(), hbm(), hbm()],
        out_specs=(vmem(),) * 4,
        scratch_shapes=[pltpu.SemaphoreType.DMA((2,))],
        compiler_params=params(16),
        cost_estimate=cost(4),
        name="maps",
    )(pos, cells, values, off_chip(states), off_chip(land_mask))

    row = lax.broadcasted_iota(jnp.int32, (3, HALO, columns), 1)
    rim = jnp.where((row < HALO // 2) == even, pair[:3], cross[:3])
    rim, cross, pair = lax.optimization_barrier((rim, cross, pair))
    rim = shifted(rim, "tm", -1)

    land, ends, *path = pl.pallas_call(
        forward_kernel,
        out_shape=(
            jax.ShapeDtypeStruct((rows, columns), f32),
            jax.ShapeDtypeStruct((3, strip, columns), f32),
        )
        + (jax.ShapeDtypeStruct((3, rows, columns), f32),) * (NSTEP + 1),
        in_specs=[smem()] + [vmem()] * 4,
        out_specs=(vmem(),) * (NSTEP + 3),
        input_output_aliases={1: 2},
        compiler_params=params(16),
        cost_estimate=cost(2),
        name="forward",
    )(pos, start, cross, pair, bits)

    previous = shifted(ends, "tm", 1)

    def adjoint(part, height, *operands):
        shapes = [jax.ShapeDtypeStruct((3, height, columns), f32)] * 2
        scratch = [pltpu.VMEM((NSTEP, 3, rows, columns), f32)]
        if part == "middle":
            shapes.append(jax.ShapeDtypeStruct((NSTEP, 3, rows, columns), f32))
            scratch = []
        return pl.pallas_call(
            adjoint_kernel(part),
            out_shape=tuple(shapes),
            in_specs=[smem()] + [vmem()] * len(operands),
            out_specs=(vmem(),) * len(shapes),
            scratch_shapes=scratch,
            compiler_params=params(24),
            cost_estimate=cost(0.1 if part == "middle" else 60),
            name="adjoint_" + part,
        )(pos, *operands)

    shared = (land, count, total, *path)
    mid_adj, mid_send, work = adjoint("middle", strip - 2 * BLK, *shared, ahead)
    mid_next = shifted(mid_send, "tm", -1)
    edge_adj, edge_send = adjoint("edge", 2 * BLK, *shared, rim, work)
    edge_next = shifted(edge_send, "tm", -1)

    def joined(middle, edge):
        return jnp.concatenate([edge[:, :BLK], middle, edge[:, BLK:]], axis=1)

    previous = jnp.where(at_first, background, previous)
    gradient = defect_weight * (states[0] - previous) + joined(mid_adj, edge_adj)
    next_state = joined(mid_next, edge_next) + share * ends
    return (gradient[None], next_state[None])


def solution(mesh):
    in_specs = (
        P("tm", None, "space", None),
        P(None, "space", None),
        P("tm", None, None),
        P("tm", None, None),
        P("space", None),
    )
    out_specs = (P("tm", None, "space", None), P("tm", None, "space", None))
    return jax.shard_map(local, mesh=mesh, in_specs=in_specs, out_specs=out_specs, check_vma=False)
```

```python
import jax
import jax.numpy as jnp
from jax import lax
from jax.experimental import pallas as pl
from jax.experimental.pallas import tpu as pltpu
from jax.sharding import PartitionSpec as P

NSTEP = 4
HALO = 8
BLK = 8

advect = 0.25
coriolis = 0.1
diffuse = 0.1
defect_weight = 2.0
obs_weight = 4.0
step_length = 0.1


def vmem():
    return pl.BlockSpec(memory_space=pltpu.VMEM)


def hbm():
    return pl.BlockSpec(memory_space=pltpu.HBM)


def off_chip(x):
    return pltpu.with_memory_space_constraint(x, pltpu.HBM)


def smem():
    return pl.BlockSpec(memory_space=pltpu.SMEM)


def east(x):
    return pltpu.roll(x, x.shape[1] - 1, axis=1)


def west(x):
    return pltpu.roll(x, 1, axis=1)


def below(x, after):
    first = lax.broadcasted_iota(jnp.int32, x.shape, 0) == 0
    return pltpu.roll(jnp.where(first, after, x), BLK - 1, axis=0)


def above(x, before):
    last = lax.broadcasted_iota(jnp.int32, x.shape, 0) == BLK - 1
    return pltpu.roll(jnp.where(last, before, x), 1, axis=0)


def prepare_kernel(
    pos_ref, states_ref, mask_ref, cells_ref, values_ref,
    cross_ref, pair_ref, seen_ref, wanted_ref, near_ref, far_ref, bits, sems
):
    strip = states_ref.shape[2]
    bottom = strip - HALO
    odd = pos_ref[3]
    copies = []
    for n, (out, at) in enumerate(((cross_ref, odd * bottom), (pair_ref, (1 - odd) * bottom))):
        at = pl.multiple_of(at, HALO)
        copies.append(
            pltpu.make_async_copy(mask_ref.at[pl.ds(at, HALO)], bits.at[n], sems.at[2 * n])
        )
        copies.append(
            pltpu.make_async_copy(
                states_ref.at[0, :, pl.ds(at, HALO)], out.at[pl.ds(0, 3)], sems.at[2 * n + 1]
            )
        )
    cut = near_ref.shape[1]
    copies.append(pltpu.make_async_copy(states_ref.at[0, :, pl.ds(0, cut)], near_ref, sems.at[6]))
    copies.append(
        pltpu.make_async_copy(states_ref.at[0, :, pl.ds(cut, strip - cut)], far_ref, sems.at[7])
    )
    copies.append(pltpu.make_async_copy(cells_ref.at[0], seen_ref, sems.at[4]))
    copies.append(pltpu.make_async_copy(values_ref.at[0], wanted_ref, sems.at[5]))
    for copy in copies:
        copy.start()
    for copy in copies:
        copy.wait()
    cross_ref[3] = bits[0].astype(jnp.float32)
    pair_ref[3] = bits[1].astype(jnp.float32)


def maps_kernel(
    pos_ref, cells_ref, values_ref, states_ref, mask_ref,
    count_ref, total_ref, start_ref, bits_ref, sems
):
    strip = mask_ref.shape[0]
    copies = (
        pltpu.make_async_copy(
            states_ref.at[0], start_ref.at[:, pl.ds(HALO, strip)], sems.at[0]
        ),
        pltpu.make_async_copy(mask_ref, bits_ref, sems.at[1]),
    )
    for copy in copies:
        copy.start()
    rows, columns = count_ref.shape[1:]
    observed = cells_ref.shape[1]
    shift = columns.bit_length() - 1
    assert columns == 1 << shift
    width = 256
    base = pos_ref[0]
    row_iota = lax.broadcasted_iota(jnp.int32, (rows, observed), 0)
    col_iota = lax.broadcasted_iota(jnp.int32, (width, observed), 0)
    for step in range(NSTEP):
        cells = cells_ref[step : step + 1, :]
        values = obs_weight * values_ref[step : step + 1, :]
        row = lax.shift_right_logical(cells, shift)
        col = cells - lax.shift_left(row, shift)
        inside = row_iota == row - base
        first = values.astype(jnp.bfloat16).astype(jnp.float32)
        rest = values - first
        second = rest.astype(jnp.bfloat16).astype(jnp.float32)
        third = rest - second
        zero = jnp.zeros((rows, observed), jnp.float32)
        parts = [
            jnp.where(inside, jnp.broadcast_to(part, (rows, observed)), zero).astype(jnp.bfloat16)
            for part in (first, second, third)
        ]
        picks = jnp.where(inside, jnp.float32(obs_weight), zero).astype(jnp.bfloat16)
        left = jnp.concatenate([picks] + parts, axis=0)
        for start in range(0, columns, width):
            hot = jnp.where(col_iota == col - start, jnp.float32(1), jnp.float32(0))
            hot = hot.astype(jnp.bfloat16)
            out = lax.dot_general(
                left, hot, (((1,), (1,)), ((), ())), preferred_element_type=jnp.float32
            )
            count_ref[step, :, start : start + width] = out[:rows]
            total_ref[step, :, start : start + width] = (
                out[rows : 2 * rows] + out[2 * rows : 3 * rows] + out[3 * rows :]
            )
    for copy in copies:
        copy.wait()


def forward_kernel(
    pos_ref, start_ref, cross_ref, pair_ref, mask_ref, land_ref, ends_ref, *path_ref
):
    strip, columns = mask_ref.shape
    rows = strip + 2 * HALO
    blocks = rows // BLK
    base = pos_ref[0]
    grid_rows = pos_ref[1]
    odd = pos_ref[3] == 1
    up = jnp.where(odd, pair_ref[...], cross_ref[...])
    down = jnp.where(odd, cross_ref[...], pair_ref[...])
    path_ref[0][:, :HALO] = up[:3]
    path_ref[0][:, HALO + strip :] = down[:3]
    land_ref[:HALO] = up[3]
    land_ref[HALO : HALO + strip] = mask_ref[...].astype(jnp.float32)
    land_ref[HALO + strip :] = down[3]

    for step in range(NSTEP):
        for i in range(blocks):
            at = slice(i * BLK, (i + 1) * BLK)
            prior = slice(max(i - 1, 0) * BLK, (max(i - 1, 0) + 1) * BLK)
            follow = slice(min(i + 1, blocks - 1) * BLK, (min(i + 1, blocks - 1) + 1) * BLK)
            h, u, v = (path_ref[step][f, at] for f in range(3))
            h0, u0, v0 = (path_ref[step][f, prior] for f in range(3))
            h2, u2, v2 = (path_ref[step][f, follow] for f in range(3))
            hn, un, vn = below(h, h2), below(u, u2), below(v, v2)
            hs, us, vs = above(h, h0), above(u, u0), above(v, v0)
            land = land_ref[at]
            half = advect / 2.0
            dh = diffuse * h
            fx = half * ((1.0 + h) * u)
            gy = half * ((1.0 + hn) * vn - (1.0 + hs) * vs)
            keep = 1.0 - 4.0 * diffuse
            h_new = keep * h + diffuse * (hn + hs) - gy + east(dh - fx) + west(dh + fx)
            du = diffuse * u
            sx = half * h
            u_new = land * (
                keep * u + coriolis * v + diffuse * (un + us) + east(du - sx) + west(du + sx)
            )
            v_new = land * (
                keep * v
                - coriolis * u
                + diffuse * (vn + vs + east(v) + west(v))
                - half * (hn - hs)
            )
            number = base + i * BLK + lax.broadcasted_iota(jnp.int32, (BLK, columns), 0)
            inside = (number >= 0) & (number < grid_rows)
            h_new = jnp.where(inside, h_new, 0.0)
            path_ref[step + 1][0, at] = h_new
            path_ref[step + 1][1, at] = u_new
            path_ref[step + 1][2, at] = v_new
    ends_ref[...] = path_ref[NSTEP][:, HALO : HALO + strip]


def near_blocks(blocks):
    return blocks // 2 + 1


def adjoint_kernel(part):
    def kernel(*refs):
        pos_ref, land_ref, count_ref, total_ref, *path_ref = refs[: NSTEP + 5]
        ahead_ref = refs[NSTEP + 5]
        out_ref, send_ref, work = refs[-3:]
        rows, columns = land_ref.shape
        blocks = rows // BLK
        last = blocks - 2
        cut = near_blocks(last)
        base = pos_ref[0]
        grid_rows = pos_ref[1]
        weight = jnp.where(pos_ref[2] == 1, 0.0, defect_weight).astype(jnp.float32)
        half = advect / 2.0
        keep = 1.0 - 4.0 * diffuse
        if part == "near":
            first, inner, final = range(1, cut + 1), range(1, cut + 1), range(2, cut)
            low, high = 1, cut
        elif part == "far":
            first, inner, final = range(cut + 1, last + 1), range(cut, last + 1), range(cut, last)
            low, high = cut - 1, last
        else:
            first, inner, final = (0, last + 1), (0, 1, last, last + 1), (1, last)
            low, high = 0, last + 1

        def get(step, f, i):
            return work[step, f, i * BLK : (i + 1) * BLK]

        def put(step, i, lam):
            at = slice(i * BLK, (i + 1) * BLK)
            number = base + i * BLK + lax.broadcasted_iota(jnp.int32, (BLK, columns), 0)
            inside = (number >= 0) & (number < grid_rows)
            force = count_ref[step, at] * path_ref[step + 1][0, at] - total_ref[step, at]
            land = land_ref[at]
            work[step, 0, at] = jnp.where(inside, lam[0] + force, 0.0)
            work[step, 1, at] = land * lam[1]
            work[step, 2, at] = land * lam[2]

        for i in first:
            at = slice(i * BLK, (i + 1) * BLK)
            if part == "edge":
                ahead = [ahead_ref[f] for f in range(3)]
            else:
                here = slice((i - first[0]) * BLK, (i - first[0] + 1) * BLK)
                ahead = [ahead_ref[f, here] for f in range(3)]
            put(
                NSTEP - 1,
                i,
                [weight * (path_ref[NSTEP][f, at] - ahead[f]) for f in range(3)],
            )

        for step in reversed(range(NSTEP)):
            for n, i in enumerate(inner if step > 0 else final):
                at = slice(i * BLK, (i + 1) * BLK)
                before, after = max(i - 1, low), min(i + 1, high)
                a, b, c = (get(step, f, i) for f in range(3))
                a0, b0, c0 = (get(step, f, before) for f in range(3))
                a2, b2, c2 = (get(step, f, after) for f in range(3))
                an, bn, cn = below(a, a2), below(b, b2), below(c, c2)
                as_, bs, cs = above(a, a0), above(b, b0), above(c, c0)
                ae, aw = east(a), west(a)
                be, bw = east(b), west(b)
                ce, cw = east(c), west(c)
                h, u, v = (path_ref[step][f, at] for f in range(3))
                fx = half * (ae - aw)
                gy = half * (an - as_)
                depth = 1.0 + h
                lh = (
                    keep * a
                    + diffuse * (ae + aw + an + as_)
                    + u * fx
                    + v * gy
                    + half * (be - bw + cn - cs)
                )
                lu = depth * fx + keep * b - coriolis * c + diffuse * (be + bw + bn + bs)
                lv = depth * gy + keep * c + coriolis * b + diffuse * (ce + cw + cn + cs)
                if step > 0:
                    put(step - 1, i, (lh, lu, lv))
                else:
                    here = slice(n * BLK, (n + 1) * BLK)
                    for f, (lam, x) in enumerate(((lh, h), (lu, u), (lv, v))):
                        out_ref[f, here] = lam
                        send_ref[f, here] = (
                            1.0 - step_length * defect_weight
                        ) * x - step_length * lam

    return kernel


def settle_kernel(places):
    def kernel(*refs):
        pos_ref, ends_ref, got_ref = refs[:3]
        out_ref, buffer, sems = refs[-3:]
        share = jnp.where(pos_ref[2] == 1, 1.0, step_length * defect_weight).astype(jnp.float32)
        copies = []
        at = 0
        for n, (low, height) in enumerate(places):
            here = slice(at, at + height)
            buffer[:, here] = got_ref[:, here] + share * ends_ref[:, low : low + height]
            copies.append(
                pltpu.make_async_copy(
                    buffer.at[:, pl.ds(at, height)],
                    out_ref.at[0, :, pl.ds(low, height)],
                    sems.at[n],
                )
            )
            copies[-1].start()
            at += height
        for copy in copies:
            copy.wait()

    return kernel


def gradient_kernel(
    pos_ref, start_ref, previous_ref, background_ref, near_ref, far_ref, edge_ref,
    out_ref, buffer, held, sems
):
    strip = out_ref.shape[2]

    def fill(source):
        def place(low, height, source_adj):
            here = slice(low, low + height)
            state = start_ref[:, HALO + low : HALO + low + height]
            buffer[:, here] = defect_weight * (state - source[:, here]) + source_adj

        cut = BLK + near_ref.shape[1]
        place(0, BLK, edge_ref[:, :BLK])
        place(BLK, near_ref.shape[1], near_ref[...])
        place(cut, far_ref.shape[1], far_ref[...])
        place(strip - BLK, BLK, edge_ref[:, BLK:])

    @pl.when(pos_ref[4] == 1)
    def _():
        copy = pltpu.make_async_copy(background_ref, held, sems.at[0])
        copy.start()
        copy.wait()
        fill(held)

    @pl.when(pos_ref[4] != 1)
    def _():
        fill(previous_ref)

    copy = pltpu.make_async_copy(buffer, out_ref.at[0], sems.at[1])
    copy.start()
    copy.wait()


def shifted(block, axis, distance):
    devices = range(lax.axis_size(axis))
    route = [(i - distance, i) for i in devices if i - distance in devices]
    return lax.ppermute(block, axis, route)


def local(states, background, obs_cells, obs_values, land_mask):
    strip, columns = states.shape[2], states.shape[3]
    rows = strip + 2 * HALO
    at_first = lax.axis_index("tm") == 0
    at_final = lax.axis_index("tm") == lax.axis_size("tm") - 1
    base = lax.axis_index("space") * strip - HALO
    odd = lax.axis_index("space") & 1
    pos = jnp.stack(
        [
            base,
            jnp.int32(strip) * lax.axis_size("space"),
            at_final.astype(jnp.int32),
            odd,
            at_first.astype(jnp.int32),
        ]
    ).astype(jnp.int32)
    f32 = jnp.float32

    def params(megabytes):
        return pltpu.CompilerParams(vmem_limit_bytes=megabytes * 1024 * 1024)

    def cost(us):
        return pl.CostEstimate(
            flops=int(us * 1.0e9), transcendentals=0, bytes_accessed=int(us * 3.0e6)
        )

    observed = obs_cells.shape[2]
    cut = near_blocks(strip // BLK) * BLK
    cross, pair, cells, values, near, far = pl.pallas_call(
        prepare_kernel,
        out_shape=(
            jax.ShapeDtypeStruct((4, HALO, columns), f32),
            jax.ShapeDtypeStruct((4, HALO, columns), f32),
            jax.ShapeDtypeStruct((NSTEP, observed), jnp.int32),
            jax.ShapeDtypeStruct((NSTEP, observed), f32),
            jax.ShapeDtypeStruct((3, cut, columns), f32),
            jax.ShapeDtypeStruct((3, strip - cut, columns), f32),
        ),
        in_specs=[smem()] + [hbm()] * 4,
        out_specs=(vmem(),) * 6,
        scratch_shapes=[
            pltpu.VMEM((2, HALO, columns), jnp.int32),
            pltpu.SemaphoreType.DMA((8,)),
        ],
        compiler_params=params(8),
        cost_estimate=cost(0.5),
        name="prepare",
    )(pos, *(off_chip(x) for x in (states, land_mask, obs_cells, obs_values)))
    cross, pair, near, far, pos, even = lax.optimization_barrier(
        (cross, pair, near, far, pos, odd == 0)
    )
    strips = lax.axis_size("space")
    inner = [(i, i ^ 1) for i in range(strips)]
    outer = [(i, j) for i in range(strips) for j in [((i + 1) ^ 1) - 1] if 0 <= j < strips]
    cross = lax.ppermute(cross, "space", outer)
    pair = lax.ppermute(pair, "space", inner)
    far = shifted(far, "tm", -1)
    near = shifted(near, "tm", -1)

    count, total, start, bits = pl.pallas_call(
        maps_kernel,
        out_shape=(
            jax.ShapeDtypeStruct((NSTEP, rows, columns), f32),
            jax.ShapeDtypeStruct((NSTEP, rows, columns), f32),
            jax.ShapeDtypeStruct((3, rows, columns), f32),
            jax.ShapeDtypeStruct((strip, columns), jnp.int32),
        ),
        in_specs=[smem(), vmem(), vmem(), hbm(), hbm()],
        out_specs=(vmem(),) * 4,
        scratch_shapes=[pltpu.SemaphoreType.DMA((2,))],
        compiler_params=params(16),
        cost_estimate=cost(4),
        name="maps",
    )(pos, cells, values, off_chip(states), off_chip(land_mask))

    row = lax.broadcasted_iota(jnp.int32, (3, HALO, columns), 1)
    rim = jnp.where((row < HALO // 2) != even, cross[:3], pair[:3])
    rim, cross, pair = lax.optimization_barrier((rim, cross, pair))
    rim = shifted(rim, "tm", -1)

    land, ends, *path = pl.pallas_call(
        forward_kernel,
        out_shape=(
            jax.ShapeDtypeStruct((rows, columns), f32),
            jax.ShapeDtypeStruct((3, strip, columns), f32),
        )
        + (jax.ShapeDtypeStruct((3, rows, columns), f32),) * (NSTEP + 1),
        in_specs=[smem()] + [vmem()] * 4,
        out_specs=(vmem(),) * (NSTEP + 3),
        input_output_aliases={1: 2},
        compiler_params=params(16),
        cost_estimate=cost(2),
        name="forward",
    )(pos, start, cross, pair, bits)

    previous = shifted(ends, "tm", 1)

    def adjoint(part, height, *operands):
        work = jax.ShapeDtypeStruct((NSTEP, 3, rows, columns), f32)
        return pl.pallas_call(
            adjoint_kernel(part),
            out_shape=(jax.ShapeDtypeStruct((3, height, columns), f32),) * 2 + (work,),
            in_specs=[smem()] + [vmem()] * len(operands),
            out_specs=(vmem(),) * 3,
            input_output_aliases={} if part == "near" else {len(operands): 2},
            compiler_params=params(24),
            cost_estimate=cost({"near": 0.1, "far": 60, "edge": 0.5}[part]),
            name="adjoint_" + part,
        )(pos, *operands)

    shared = (land, count, total, *path)
    first, near_send, work = adjoint("near", cut - 2 * BLK, *shared, near)
    second, far_send, work = adjoint("far", strip - cut, *shared, far, work)
    outer, edge_send, work = adjoint("edge", 2 * BLK, *shared, rim, work)
    edge_sent = shifted(edge_send, "tm", -1)
    far_sent = shifted(far_send, "tm", -1)
    near_sent = shifted(near_send, "tm", -1)

    def settle(name, places, arrived, *held):
        height = arrived.shape[1]
        return pl.pallas_call(
            settle_kernel(places),
            out_shape=jax.ShapeDtypeStruct(states.shape, f32),
            in_specs=[smem()] + [vmem()] * 2 + [hbm()] * len(held),
            out_specs=hbm(),
            scratch_shapes=[
                pltpu.VMEM((3, height, columns), f32),
                pltpu.SemaphoreType.DMA((len(places),)),
            ],
            input_output_aliases={3: 0} if held else {},
            compiler_params=params(8),
            cost_estimate=cost(0.01),
            name="settle_" + name,
        )(pos, ends, arrived, *(off_chip(x) for x in held))

    gradient = pl.pallas_call(
        gradient_kernel,
        out_shape=jax.ShapeDtypeStruct(states.shape, f32),
        in_specs=[smem(), vmem(), vmem(), hbm(), vmem(), vmem(), vmem()],
        out_specs=hbm(),
        scratch_shapes=[
            pltpu.VMEM((3, strip, columns), f32),
            pltpu.VMEM((3, strip, columns), f32),
            pltpu.SemaphoreType.DMA((2,)),
        ],
        compiler_params=params(12),
        cost_estimate=cost(0.01),
        name="gradient",
    )(pos, path[0], previous, off_chip(background), first, second, outer)
    next_state = settle("near", [(BLK, cut - 2 * BLK)], near_sent)
    next_state = settle("far", [(cut - BLK, strip - cut)], far_sent, next_state, gradient)
    next_state = settle("edge", [(0, BLK), (strip - BLK, BLK)], edge_sent, next_state)
    return (gradient, next_state)


def solution(mesh):
    in_specs = (
        P("tm", None, "space", None),
        P(None, "space", None),
        P("tm", None, None),
        P("tm", None, None),
        P("space", None),
    )
    out_specs = (P("tm", None, "space", None), P("tm", None, "space", None))
    return jax.shard_map(local, mesh=mesh, in_specs=in_specs, out_specs=out_specs, check_vma=False)
```

```python
import jax
import jax.numpy as jnp
from jax import lax
from jax.experimental import pallas as pl
from jax.experimental.pallas import tpu as pltpu
from jax.sharding import PartitionSpec as P

NSTEP = 4
HALO = 8
BLK = 8
RING = 8

advect = 0.25
coriolis = 0.1
diffuse = 0.1
defect_weight = 2.0
obs_weight = 4.0
step_length = 0.1


def vmem():
    return pl.BlockSpec(memory_space=pltpu.VMEM)


def hbm():
    return pl.BlockSpec(memory_space=pltpu.HBM)


def off_chip(x):
    return pltpu.with_memory_space_constraint(x, pltpu.HBM)


def smem():
    return pl.BlockSpec(memory_space=pltpu.SMEM)


def east(x):
    return pltpu.roll(x, x.shape[1] - 1, axis=1)


def west(x):
    return pltpu.roll(x, 1, axis=1)


def below(x, after):
    first = lax.broadcasted_iota(jnp.int32, x.shape, 0) == 0
    return pltpu.roll(jnp.where(first, after, x), BLK - 1, axis=0)


def above(x, before):
    last = lax.broadcasted_iota(jnp.int32, x.shape, 0) == BLK - 1
    return pltpu.roll(jnp.where(last, before, x), 1, axis=0)


def fill_maps(pos_ref, cells_ref, values_ref, count_ref, total_ref):
    rows, columns = count_ref.shape[1:]
    observed = cells_ref.shape[1]
    shift = columns.bit_length() - 1
    assert columns == 1 << shift
    width = 256
    base = pos_ref[0]
    row_iota = lax.broadcasted_iota(jnp.int32, (rows, observed), 0)
    col_iota = lax.broadcasted_iota(jnp.int32, (width, observed), 0)
    for step in range(NSTEP):
        cells = cells_ref[step : step + 1, :]
        values = obs_weight * values_ref[step : step + 1, :]
        row = lax.shift_right_logical(cells, shift)
        col = cells - lax.shift_left(row, shift)
        inside = row_iota == row - base
        first = values.astype(jnp.bfloat16).astype(jnp.float32)
        rest = values - first
        second = rest.astype(jnp.bfloat16).astype(jnp.float32)
        third = rest - second
        zero = jnp.zeros((rows, observed), jnp.float32)
        parts = [
            jnp.where(inside, jnp.broadcast_to(part, (rows, observed)), zero).astype(jnp.bfloat16)
            for part in (first, second, third)
        ]
        picks = jnp.where(inside, jnp.float32(obs_weight), zero).astype(jnp.bfloat16)
        left = jnp.concatenate([picks] + parts, axis=0)
        for start in range(0, columns, width):
            hot = jnp.where(col_iota == col - start, jnp.float32(1), jnp.float32(0))
            hot = hot.astype(jnp.bfloat16)
            out = lax.dot_general(
                left, hot, (((1,), (1,)), ((), ())), preferred_element_type=jnp.float32
            )
            count_ref[step, :, start : start + width] = out[:rows]
            total_ref[step, :, start : start + width] = (
                out[rows : 2 * rows] + out[2 * rows : 3 * rows] + out[3 * rows :]
            )


def maps_kernel(
    pos_ref, cells_ref, values_ref, states_ref, mask_ref, early_count_ref, early_total_ref,
    count_ref, total_ref, start_ref, bits_ref, sems
):
    strip = mask_ref.shape[0]
    copies = (
        pltpu.make_async_copy(
            states_ref.at[0], start_ref.at[:, pl.ds(HALO, strip)], sems.at[0]
        ),
        pltpu.make_async_copy(mask_ref, bits_ref, sems.at[1]),
    )
    for copy in copies:
        copy.start()

    @pl.when(pos_ref[5] == 0)
    def _():
        fill_maps(pos_ref, cells_ref, values_ref, count_ref, total_ref)

    for copy in copies:
        copy.wait()


def prepare_kernel(
    pos_ref, states_ref, mask_ref, cells_ref, values_ref,
    cross_ref, pair_ref, seen_ref, wanted_ref, near_ref, far_ref, count_ref, total_ref, bits, sems
):
    strip = states_ref.shape[2]
    bottom = strip - HALO
    odd = pos_ref[3]
    copies = []
    for n, (out, at) in enumerate(((cross_ref, odd * bottom), (pair_ref, (1 - odd) * bottom))):
        at = pl.multiple_of(at, HALO)
        copies.append(
            pltpu.make_async_copy(mask_ref.at[pl.ds(at, HALO)], bits.at[n], sems.at[2 * n])
        )
        copies.append(
            pltpu.make_async_copy(
                states_ref.at[0, :, pl.ds(at, HALO)], out.at[pl.ds(0, 3)], sems.at[2 * n + 1]
            )
        )
    cut = near_ref.shape[1]
    copies.append(pltpu.make_async_copy(states_ref.at[0, :, pl.ds(0, cut)], near_ref, sems.at[6]))
    copies.append(
        pltpu.make_async_copy(states_ref.at[0, :, pl.ds(cut, strip - cut)], far_ref, sems.at[7])
    )
    copies.append(pltpu.make_async_copy(cells_ref.at[0], seen_ref, sems.at[4]))
    copies.append(pltpu.make_async_copy(values_ref.at[0], wanted_ref, sems.at[5]))
    for copy in copies:
        copy.start()
    for copy in copies:
        copy.wait()
    cross_ref[3] = bits[0].astype(jnp.float32)
    pair_ref[3] = bits[1].astype(jnp.float32)

    @pl.when(pos_ref[5] != 0)
    def _():
        fill_maps(pos_ref, seen_ref, wanted_ref, count_ref, total_ref)


def forward_kernel(
    pos_ref, start_ref, cross_ref, pair_ref, mask_ref, land_ref, ends_ref, *path_ref
):
    strip, columns = mask_ref.shape
    rows = strip + 2 * HALO
    blocks = rows // BLK
    base = pos_ref[0]
    grid_rows = pos_ref[1]
    odd = pos_ref[3] == 1
    up = jnp.where(odd, pair_ref[...], cross_ref[...])
    down = jnp.where(odd, cross_ref[...], pair_ref[...])
    path_ref[0][:, :HALO] = up[:3]
    path_ref[0][:, HALO + strip :] = down[:3]
    land_ref[:HALO] = up[3]
    land_ref[HALO : HALO + strip] = mask_ref[...].astype(jnp.float32)
    land_ref[HALO + strip :] = down[3]

    for step in range(NSTEP):
        for i in range(blocks):
            at = slice(i * BLK, (i + 1) * BLK)
            prior = slice(max(i - 1, 0) * BLK, (max(i - 1, 0) + 1) * BLK)
            follow = slice(min(i + 1, blocks - 1) * BLK, (min(i + 1, blocks - 1) + 1) * BLK)
            h, u, v = (path_ref[step][f, at] for f in range(3))
            h0, u0, v0 = (path_ref[step][f, prior] for f in range(3))
            h2, u2, v2 = (path_ref[step][f, follow] for f in range(3))
            hn, un, vn = below(h, h2), below(u, u2), below(v, v2)
            hs, us, vs = above(h, h0), above(u, u0), above(v, v0)
            land = land_ref[at]
            half = advect / 2.0
            dh = diffuse * h
            fx = half * ((1.0 + h) * u)
            gy = half * ((1.0 + hn) * vn - (1.0 + hs) * vs)
            keep = 1.0 - 4.0 * diffuse
            h_new = keep * h + diffuse * (hn + hs) - gy + east(dh - fx) + west(dh + fx)
            du = diffuse * u
            sx = half * h
            u_new = land * (
                keep * u + coriolis * v + diffuse * (un + us) + east(du - sx) + west(du + sx)
            )
            v_new = land * (
                keep * v
                - coriolis * u
                + diffuse * (vn + vs + east(v) + west(v))
                - half * (hn - hs)
            )
            number = base + i * BLK + lax.broadcasted_iota(jnp.int32, (BLK, columns), 0)
            inside = (number >= 0) & (number < grid_rows)
            h_new = jnp.where(inside, h_new, 0.0)
            path_ref[step + 1][0, at] = h_new
            path_ref[step + 1][1, at] = u_new
            path_ref[step + 1][2, at] = v_new
    ends_ref[...] = path_ref[NSTEP][:, HALO : HALO + strip]


def near_blocks(blocks):
    return blocks // 2 + 1


def adjoint_kernel(part):
    def kernel(*refs):
        pos_ref, land_ref, count_ref, total_ref, *path_ref = refs[: NSTEP + 5]
        ahead_ref = refs[NSTEP + 5]
        out_ref, send_ref, work = refs[-3:]
        rows, columns = land_ref.shape
        blocks = rows // BLK
        last = blocks - 2
        cut = near_blocks(last)
        base = pos_ref[0]
        grid_rows = pos_ref[1]
        weight = jnp.where(pos_ref[2] == 1, 0.0, defect_weight).astype(jnp.float32)
        half = advect / 2.0
        keep = 1.0 - 4.0 * diffuse
        if part == "near":
            first, inner, final = range(1, cut + 1), range(1, cut + 1), range(2, cut)
            low, high = 1, cut
        elif part == "far":
            first, inner, final = range(cut + 1, last + 1), range(cut, last + 1), range(cut, last)
            low, high = cut - 1, last
        else:
            first, inner, final = (0, last + 1), (0, 1, last, last + 1), (1, last)
            low, high = 0, last + 1

        def get(step, f, i):
            return work[step, f, i * BLK : (i + 1) * BLK]

        def put(step, i, lam):
            at = slice(i * BLK, (i + 1) * BLK)
            number = base + i * BLK + lax.broadcasted_iota(jnp.int32, (BLK, columns), 0)
            inside = (number >= 0) & (number < grid_rows)
            force = count_ref[step, at] * path_ref[step + 1][0, at] - total_ref[step, at]
            land = land_ref[at]
            work[step, 0, at] = jnp.where(inside, lam[0] + force, 0.0)
            work[step, 1, at] = land * lam[1]
            work[step, 2, at] = land * lam[2]

        for i in first:
            at = slice(i * BLK, (i + 1) * BLK)
            if part == "edge":
                ahead = [ahead_ref[f] for f in range(3)]
            else:
                here = slice((i - first[0]) * BLK, (i - first[0] + 1) * BLK)
                ahead = [ahead_ref[f, here] for f in range(3)]
            put(
                NSTEP - 1,
                i,
                [weight * (path_ref[NSTEP][f, at] - ahead[f]) for f in range(3)],
            )

        for step in reversed(range(NSTEP)):
            for n, i in enumerate(inner if step > 0 else final):
                at = slice(i * BLK, (i + 1) * BLK)
                before, after = max(i - 1, low), min(i + 1, high)
                a, b, c = (get(step, f, i) for f in range(3))
                a0, b0, c0 = (get(step, f, before) for f in range(3))
                a2, b2, c2 = (get(step, f, after) for f in range(3))
                an, bn, cn = below(a, a2), below(b, b2), below(c, c2)
                as_, bs, cs = above(a, a0), above(b, b0), above(c, c0)
                ae, aw = east(a), west(a)
                be, bw = east(b), west(b)
                ce, cw = east(c), west(c)
                h, u, v = (path_ref[step][f, at] for f in range(3))
                fx = half * (ae - aw)
                gy = half * (an - as_)
                depth = 1.0 + h
                lh = (
                    keep * a
                    + diffuse * (ae + aw + an + as_)
                    + u * fx
                    + v * gy
                    + half * (be - bw + cn - cs)
                )
                lu = depth * fx + keep * b - coriolis * c + diffuse * (be + bw + bn + bs)
                lv = depth * gy + keep * c + coriolis * b + diffuse * (ce + cw + cn + cs)
                if step > 0:
                    put(step - 1, i, (lh, lu, lv))
                else:
                    here = slice(n * BLK, (n + 1) * BLK)
                    for f, (lam, x) in enumerate(((lh, h), (lu, u), (lv, v))):
                        out_ref[f, here] = lam
                        send_ref[f, here] = (
                            1.0 - step_length * defect_weight
                        ) * x - step_length * lam

    return kernel


def settle_kernel(places):
    def kernel(*refs):
        pos_ref, ends_ref, got_ref = refs[:3]
        out_ref, buffer, sems = refs[-3:]
        share = jnp.where(pos_ref[2] == 1, 1.0, step_length * defect_weight).astype(jnp.float32)
        copies = []
        at = 0
        for n, (low, height) in enumerate(places):
            here = slice(at, at + height)
            buffer[:, here] = got_ref[:, here] + share * ends_ref[:, low : low + height]
            copies.append(
                pltpu.make_async_copy(
                    buffer.at[:, pl.ds(at, height)],
                    out_ref.at[0, :, pl.ds(low, height)],
                    sems.at[n],
                )
            )
            copies[-1].start()
            at += height
        for copy in copies:
            copy.wait()

    return kernel


def gradient_kernel(
    pos_ref, start_ref, previous_ref, background_ref, near_ref, far_ref, edge_ref,
    out_ref, buffer, held, sems
):
    strip = out_ref.shape[2]

    def fill(source):
        def place(low, height, source_adj):
            here = slice(low, low + height)
            state = start_ref[:, HALO + low : HALO + low + height]
            buffer[:, here] = defect_weight * (state - source[:, here]) + source_adj

        cut = BLK + near_ref.shape[1]
        place(0, BLK, edge_ref[:, :BLK])
        place(BLK, near_ref.shape[1], near_ref[...])
        place(cut, far_ref.shape[1], far_ref[...])
        place(strip - BLK, BLK, edge_ref[:, BLK:])

    @pl.when(pos_ref[4] == 1)
    def _():
        copy = pltpu.make_async_copy(background_ref, held, sems.at[0])
        copy.start()
        copy.wait()
        fill(held)

    @pl.when(pos_ref[4] != 1)
    def _():
        fill(previous_ref)

    copy = pltpu.make_async_copy(buffer, out_ref.at[0], sems.at[1])
    copy.start()
    copy.wait()


def shifted(block, axis, distance):
    devices = range(lax.axis_size(axis))
    route = [(i - distance, i) for i in devices if i - distance in devices]
    return lax.ppermute(block, axis, route)


def local(states, background, obs_cells, obs_values, land_mask):
    strip, columns = states.shape[2], states.shape[3]
    rows = strip + 2 * HALO
    at_first = lax.axis_index("tm") == 0
    at_final = lax.axis_index("tm") == lax.axis_size("tm") - 1
    base = lax.axis_index("space") * strip - HALO
    odd = lax.axis_index("space") & 1
    pos = jnp.stack(
        [
            base,
            jnp.int32(strip) * lax.axis_size("space"),
            at_final.astype(jnp.int32),
            odd,
            at_first.astype(jnp.int32),
            ((lax.axis_index("tm") & (RING - 1) < 2) & (lax.axis_index("tm") >= RING)).astype(jnp.int32),
        ]
    ).astype(jnp.int32)
    f32 = jnp.float32

    def params(megabytes):
        return pltpu.CompilerParams(vmem_limit_bytes=megabytes * 1024 * 1024)

    def cost(us):
        return pl.CostEstimate(
            flops=int(us * 1.0e9), transcendentals=0, bytes_accessed=int(us * 3.0e6)
        )

    observed = obs_cells.shape[2]
    cut = near_blocks(strip // BLK) * BLK
    cross, pair, cells, values, near, far, count, total = pl.pallas_call(
        prepare_kernel,
        out_shape=(
            jax.ShapeDtypeStruct((4, HALO, columns), f32),
            jax.ShapeDtypeStruct((4, HALO, columns), f32),
            jax.ShapeDtypeStruct((NSTEP, observed), jnp.int32),
            jax.ShapeDtypeStruct((NSTEP, observed), f32),
            jax.ShapeDtypeStruct((3, cut, columns), f32),
            jax.ShapeDtypeStruct((3, strip - cut, columns), f32),
            jax.ShapeDtypeStruct((NSTEP, rows, columns), f32),
            jax.ShapeDtypeStruct((NSTEP, rows, columns), f32),
        ),
        in_specs=[smem()] + [hbm()] * 4,
        out_specs=(vmem(),) * 8,
        scratch_shapes=[
            pltpu.VMEM((2, HALO, columns), jnp.int32),
            pltpu.SemaphoreType.DMA((8,)),
        ],
        compiler_params=params(16),
        cost_estimate=cost(0.5),
        name="prepare",
    )(pos, *(off_chip(x) for x in (states, land_mask, obs_cells, obs_values)))
    cross, pair, near, far, pos, even = lax.optimization_barrier(
        (cross, pair, near, far, pos, odd == 0)
    )
    strips = lax.axis_size("space")
    inner = [(i, i ^ 1) for i in range(strips)]
    outer = [(i, j) for i in range(strips) for j in [((i + 1) ^ 1) - 1] if 0 <= j < strips]
    cross = lax.ppermute(cross, "space", outer)
    pair = lax.ppermute(pair, "space", inner)
    far = shifted(far, "tm", -1)
    near = shifted(near, "tm", -1)

    count, total, start, bits = pl.pallas_call(
        maps_kernel,
        out_shape=(
            jax.ShapeDtypeStruct((NSTEP, rows, columns), f32),
            jax.ShapeDtypeStruct((NSTEP, rows, columns), f32),
            jax.ShapeDtypeStruct((3, rows, columns), f32),
            jax.ShapeDtypeStruct((strip, columns), jnp.int32),
        ),
        in_specs=[smem(), vmem(), vmem(), hbm(), hbm(), vmem(), vmem()],
        out_specs=(vmem(),) * 4,
        input_output_aliases={5: 0, 6: 1},
        scratch_shapes=[pltpu.SemaphoreType.DMA((2,))],
        compiler_params=params(16),
        cost_estimate=cost(4),
        name="maps",
    )(pos, cells, values, off_chip(states), off_chip(land_mask), count, total)

    row = lax.broadcasted_iota(jnp.int32, (3, HALO, columns), 1)
    rim = jnp.where((row < HALO // 2) != even, cross[:3], pair[:3])
    rim, cross, pair = lax.optimization_barrier((rim, cross, pair))
    rim = shifted(rim, "tm", -1)

    land, ends, *path = pl.pallas_call(
        forward_kernel,
        out_shape=(
            jax.ShapeDtypeStruct((rows, columns), f32),
            jax.ShapeDtypeStruct((3, strip, columns), f32),
        )
        + (jax.ShapeDtypeStruct((3, rows, columns), f32),) * (NSTEP + 1),
        in_specs=[smem()] + [vmem()] * 4,
        out_specs=(vmem(),) * (NSTEP + 3),
        input_output_aliases={1: 2},
        compiler_params=params(16),
        cost_estimate=cost(2),
        name="forward",
    )(pos, start, cross, pair, bits)

    previous = shifted(ends, "tm", 1)

    def adjoint(part, height, *operands):
        work = jax.ShapeDtypeStruct((NSTEP, 3, rows, columns), f32)
        return pl.pallas_call(
            adjoint_kernel(part),
            out_shape=(jax.ShapeDtypeStruct((3, height, columns), f32),) * 2 + (work,),
            in_specs=[smem()] + [vmem()] * len(operands),
            out_specs=(vmem(),) * 3,
            input_output_aliases={} if part == "near" else {len(operands): 2},
            compiler_params=params(24),
            cost_estimate=cost({"near": 0.1, "far": 60, "edge": 0.5}[part]),
            name="adjoint_" + part,
        )(pos, *operands)

    shared = (land, count, total, *path)
    first, near_send, work = adjoint("near", cut - 2 * BLK, *shared, near)
    second, far_send, work = adjoint("far", strip - cut, *shared, far, work)
    outer, edge_send, work = adjoint("edge", 2 * BLK, *shared, rim, work)
    edge_sent = shifted(edge_send, "tm", -1)
    far_sent = shifted(far_send, "tm", -1)
    near_sent = shifted(near_send, "tm", -1)

    def settle(name, places, arrived, *held):
        height = arrived.shape[1]
        return pl.pallas_call(
            settle_kernel(places),
            out_shape=jax.ShapeDtypeStruct(states.shape, f32),
            in_specs=[smem()] + [vmem()] * 2 + [hbm()] * len(held),
            out_specs=hbm(),
            scratch_shapes=[
                pltpu.VMEM((3, height, columns), f32),
                pltpu.SemaphoreType.DMA((len(places),)),
            ],
            input_output_aliases={3: 0} if held else {},
            compiler_params=params(8),
            cost_estimate=cost(0.01),
            name="settle_" + name,
        )(pos, ends, arrived, *(off_chip(x) for x in held))

    gradient = pl.pallas_call(
        gradient_kernel,
        out_shape=jax.ShapeDtypeStruct(states.shape, f32),
        in_specs=[smem(), vmem(), vmem(), hbm(), vmem(), vmem(), vmem()],
        out_specs=hbm(),
        scratch_shapes=[
            pltpu.VMEM((3, strip, columns), f32),
            pltpu.VMEM((3, strip, columns), f32),
            pltpu.SemaphoreType.DMA((2,)),
        ],
        compiler_params=params(12),
        cost_estimate=cost(0.01),
        name="gradient",
    )(pos, path[0], previous, off_chip(background), first, second, outer)
    next_state = settle("near", [(BLK, cut - 2 * BLK)], near_sent)
    next_state = settle("far", [(cut - BLK, strip - cut)], far_sent, next_state)
    next_state = settle("edge", [(0, BLK), (strip - BLK, BLK)], edge_sent, next_state, gradient)
    return (gradient, next_state)


def solution(mesh):
    in_specs = (
        P("tm", None, "space", None),
        P(None, "space", None),
        P("tm", None, None),
        P("tm", None, None),
        P("space", None),
    )
    out_specs = (P("tm", None, "space", None), P("tm", None, "space", None))
    return jax.shard_map(local, mesh=mesh, in_specs=in_specs, out_specs=out_specs, check_vma=False)
```

```python
import jax
import jax.numpy as jnp
from jax import lax
from jax.experimental import pallas as pl
from jax.experimental.pallas import tpu as pltpu
from jax.sharding import PartitionSpec as P

NSTEP = 4
HALO = 8
BLK = 8
RING = 8

advect = 0.25
coriolis = 0.1
diffuse = 0.1
defect_weight = 2.0
obs_weight = 4.0
step_length = 0.1


def vmem():
    return pl.BlockSpec(memory_space=pltpu.VMEM)


def hbm():
    return pl.BlockSpec(memory_space=pltpu.HBM)


def off_chip(x):
    return pltpu.with_memory_space_constraint(x, pltpu.HBM)


def smem():
    return pl.BlockSpec(memory_space=pltpu.SMEM)


def east(x):
    return pltpu.roll(x, x.shape[1] - 1, axis=1)


def west(x):
    return pltpu.roll(x, 1, axis=1)


def below(x, after):
    first = lax.broadcasted_iota(jnp.int32, x.shape, 0) == 0
    return pltpu.roll(jnp.where(first, after, x), BLK - 1, axis=0)


def above(x, before):
    last = lax.broadcasted_iota(jnp.int32, x.shape, 0) == BLK - 1
    return pltpu.roll(jnp.where(last, before, x), 1, axis=0)


def fill_maps(pos_ref, cells_ref, values_ref, count_ref, total_ref):
    rows, columns = count_ref.shape[1:]
    observed = cells_ref.shape[1]
    shift = columns.bit_length() - 1
    assert columns == 1 << shift
    width = 256
    base = pos_ref[0]
    row_iota = lax.broadcasted_iota(jnp.int32, (rows, observed), 0)
    col_iota = lax.broadcasted_iota(jnp.int32, (width, observed), 0)
    for step in range(NSTEP):
        cells = cells_ref[step : step + 1, :]
        values = obs_weight * values_ref[step : step + 1, :]
        row = lax.shift_right_logical(cells, shift)
        col = cells - lax.shift_left(row, shift)
        inside = row_iota == row - base
        first = values.astype(jnp.bfloat16).astype(jnp.float32)
        rest = values - first
        second = rest.astype(jnp.bfloat16).astype(jnp.float32)
        third = rest - second
        zero = jnp.zeros((rows, observed), jnp.float32)
        parts = [
            jnp.where(inside, jnp.broadcast_to(part, (rows, observed)), zero).astype(jnp.bfloat16)
            for part in (first, second, third)
        ]
        picks = jnp.where(inside, jnp.float32(obs_weight), zero).astype(jnp.bfloat16)
        left = jnp.concatenate([picks] + parts, axis=0)
        for start in range(0, columns, width):
            hot = jnp.where(col_iota == col - start, jnp.float32(1), jnp.float32(0))
            hot = hot.astype(jnp.bfloat16)
            out = lax.dot_general(
                left, hot, (((1,), (1,)), ((), ())), preferred_element_type=jnp.float32
            )
            count_ref[step, :, start : start + width] = out[:rows]
            total_ref[step, :, start : start + width] = (
                out[rows : 2 * rows] + out[2 * rows : 3 * rows] + out[3 * rows :]
            )


def maps_kernel(
    pos_ref, cells_ref, values_ref, states_ref, mask_ref, early_count_ref, early_total_ref,
    count_ref, total_ref, start_ref, bits_ref, sems
):
    strip = mask_ref.shape[0]
    copies = (
        pltpu.make_async_copy(
            states_ref.at[0], start_ref.at[:, pl.ds(HALO, strip)], sems.at[0]
        ),
        pltpu.make_async_copy(mask_ref, bits_ref, sems.at[1]),
    )
    for copy in copies:
        copy.start()

    @pl.when(pos_ref[5] == 0)
    def _():
        fill_maps(pos_ref, cells_ref, values_ref, count_ref, total_ref)

    for copy in copies:
        copy.wait()


def prepare_kernel(
    pos_ref, states_ref, mask_ref, cells_ref, values_ref,
    cross_ref, pair_ref, seen_ref, wanted_ref, near_ref, far_ref, count_ref, total_ref, bits, sems
):
    strip = states_ref.shape[2]
    bottom = strip - HALO
    odd = pos_ref[3]
    copies = []
    for n, (out, at) in enumerate(((cross_ref, odd * bottom), (pair_ref, (1 - odd) * bottom))):
        at = pl.multiple_of(at, HALO)
        copies.append(
            pltpu.make_async_copy(mask_ref.at[pl.ds(at, HALO)], bits.at[n], sems.at[2 * n])
        )
        copies.append(
            pltpu.make_async_copy(
                states_ref.at[0, :, pl.ds(at, HALO)], out.at[pl.ds(0, 3)], sems.at[2 * n + 1]
            )
        )
    cut = near_ref.shape[1]
    copies.append(pltpu.make_async_copy(states_ref.at[0, :, pl.ds(0, cut)], near_ref, sems.at[6]))
    copies.append(
        pltpu.make_async_copy(states_ref.at[0, :, pl.ds(cut, strip - cut)], far_ref, sems.at[7])
    )
    copies.append(pltpu.make_async_copy(cells_ref.at[0], seen_ref, sems.at[4]))
    copies.append(pltpu.make_async_copy(values_ref.at[0], wanted_ref, sems.at[5]))
    for copy in copies:
        copy.start()
    for copy in copies:
        copy.wait()
    cross_ref[3] = bits[0].astype(jnp.float32)
    pair_ref[3] = bits[1].astype(jnp.float32)

    @pl.when(pos_ref[5] != 0)
    def _():
        fill_maps(pos_ref, seen_ref, wanted_ref, count_ref, total_ref)


def forward(pos_ref, cross_ref, pair_ref, mask_ref, land_ref, ends_ref, path_ref):
    strip, columns = mask_ref.shape
    rows = strip + 2 * HALO
    blocks = rows // BLK
    base = pos_ref[0]
    grid_rows = pos_ref[1]
    odd = pos_ref[3] == 1
    up = jnp.where(odd, pair_ref[...], cross_ref[...])
    down = jnp.where(odd, cross_ref[...], pair_ref[...])
    path_ref[0][:, :HALO] = up[:3]
    path_ref[0][:, HALO + strip :] = down[:3]
    land_ref[:HALO] = up[3]
    land_ref[HALO : HALO + strip] = mask_ref[...].astype(jnp.float32)
    land_ref[HALO + strip :] = down[3]

    for step in range(NSTEP):
        for i in range(blocks):
            at = slice(i * BLK, (i + 1) * BLK)
            prior = slice(max(i - 1, 0) * BLK, (max(i - 1, 0) + 1) * BLK)
            follow = slice(min(i + 1, blocks - 1) * BLK, (min(i + 1, blocks - 1) + 1) * BLK)
            h, u, v = (path_ref[step][f, at] for f in range(3))
            h0, u0, v0 = (path_ref[step][f, prior] for f in range(3))
            h2, u2, v2 = (path_ref[step][f, follow] for f in range(3))
            hn, un, vn = below(h, h2), below(u, u2), below(v, v2)
            hs, us, vs = above(h, h0), above(u, u0), above(v, v0)
            land = land_ref[at]
            half = advect / 2.0
            dh = diffuse * h
            fx = half * ((1.0 + h) * u)
            gy = half * ((1.0 + hn) * vn - (1.0 + hs) * vs)
            keep = 1.0 - 4.0 * diffuse
            h_new = keep * h + diffuse * (hn + hs) - gy + east(dh - fx) + west(dh + fx)
            du = diffuse * u
            sx = half * h
            u_new = land * (
                keep * u + coriolis * v + diffuse * (un + us) + east(du - sx) + west(du + sx)
            )
            v_new = land * (
                keep * v
                - coriolis * u
                + diffuse * (vn + vs + east(v) + west(v))
                - half * (hn - hs)
            )
            number = base + i * BLK + lax.broadcasted_iota(jnp.int32, (BLK, columns), 0)
            inside = (number >= 0) & (number < grid_rows)
            h_new = jnp.where(inside, h_new, 0.0)
            path_ref[step + 1][0, at] = h_new
            path_ref[step + 1][1, at] = u_new
            path_ref[step + 1][2, at] = v_new
    ends_ref[...] = path_ref[NSTEP][:, HALO : HALO + strip]


def forward_kernel(early):
    def kernel(*refs):
        pos_ref, start_ref, cross_ref, pair_ref, mask_ref = refs[:5]
        land_ref, ends_ref, *path_ref = refs[-(NSTEP + 3) :]

        @pl.when(pos_ref[5] == (1 if early else 0))
        def _():
            forward(pos_ref, cross_ref, pair_ref, mask_ref, land_ref, ends_ref, path_ref)

    return kernel


def near_blocks(blocks):
    return blocks // 2 + 1


def adjoint_kernel(part):
    def kernel(*refs):
        pos_ref, land_ref, count_ref, total_ref, *path_ref = refs[: NSTEP + 5]
        ahead_ref = refs[NSTEP + 5]
        out_ref, send_ref, work = refs[-3:]
        rows, columns = land_ref.shape
        blocks = rows // BLK
        last = blocks - 2
        cut = near_blocks(last)
        base = pos_ref[0]
        grid_rows = pos_ref[1]
        weight = jnp.where(pos_ref[2] == 1, 0.0, defect_weight).astype(jnp.float32)
        half = advect / 2.0
        keep = 1.0 - 4.0 * diffuse
        if part == "near":
            first, inner, final = range(1, cut + 1), range(1, cut + 1), range(2, cut)
            low, high = 1, cut
        elif part == "far":
            first, inner, final = range(cut + 1, last + 1), range(cut, last + 1), range(cut, last)
            low, high = cut - 1, last
        else:
            first, inner, final = (0, last + 1), (0, 1, last, last + 1), (1, last)
            low, high = 0, last + 1

        def get(step, f, i):
            return work[step, f, i * BLK : (i + 1) * BLK]

        def put(step, i, lam):
            at = slice(i * BLK, (i + 1) * BLK)
            number = base + i * BLK + lax.broadcasted_iota(jnp.int32, (BLK, columns), 0)
            inside = (number >= 0) & (number < grid_rows)
            force = count_ref[step, at] * path_ref[step + 1][0, at] - total_ref[step, at]
            land = land_ref[at]
            work[step, 0, at] = jnp.where(inside, lam[0] + force, 0.0)
            work[step, 1, at] = land * lam[1]
            work[step, 2, at] = land * lam[2]

        for i in first:
            at = slice(i * BLK, (i + 1) * BLK)
            if part == "edge":
                ahead = [ahead_ref[f] for f in range(3)]
            else:
                here = slice((i - first[0]) * BLK, (i - first[0] + 1) * BLK)
                ahead = [ahead_ref[f, here] for f in range(3)]
            put(
                NSTEP - 1,
                i,
                [weight * (path_ref[NSTEP][f, at] - ahead[f]) for f in range(3)],
            )

        for step in reversed(range(NSTEP)):
            for n, i in enumerate(inner if step > 0 else final):
                at = slice(i * BLK, (i + 1) * BLK)
                before, after = max(i - 1, low), min(i + 1, high)
                a, b, c = (get(step, f, i) for f in range(3))
                a0, b0, c0 = (get(step, f, before) for f in range(3))
                a2, b2, c2 = (get(step, f, after) for f in range(3))
                an, bn, cn = below(a, a2), below(b, b2), below(c, c2)
                as_, bs, cs = above(a, a0), above(b, b0), above(c, c0)
                ae, aw = east(a), west(a)
                be, bw = east(b), west(b)
                ce, cw = east(c), west(c)
                h, u, v = (path_ref[step][f, at] for f in range(3))
                fx = half * (ae - aw)
                gy = half * (an - as_)
                depth = 1.0 + h
                lh = (
                    keep * a
                    + diffuse * (ae + aw + an + as_)
                    + u * fx
                    + v * gy
                    + half * (be - bw + cn - cs)
                )
                lu = depth * fx + keep * b - coriolis * c + diffuse * (be + bw + bn + bs)
                lv = depth * gy + keep * c + coriolis * b + diffuse * (ce + cw + cn + cs)
                if step > 0:
                    put(step - 1, i, (lh, lu, lv))
                else:
                    here = slice(n * BLK, (n + 1) * BLK)
                    for f, (lam, x) in enumerate(((lh, h), (lu, u), (lv, v))):
                        out_ref[f, here] = lam
                        send_ref[f, here] = (
                            1.0 - step_length * defect_weight
                        ) * x - step_length * lam

    return kernel


def settle_kernel(places):
    def kernel(*refs):
        pos_ref, ends_ref, got_ref = refs[:3]
        out_ref, buffer, sems = refs[-3:]
        share = jnp.where(pos_ref[2] == 1, 1.0, step_length * defect_weight).astype(jnp.float32)
        copies = []
        at = 0
        for n, (low, height) in enumerate(places):
            here = slice(at, at + height)
            buffer[:, here] = got_ref[:, here] + share * ends_ref[:, low : low + height]
            copies.append(
                pltpu.make_async_copy(
                    buffer.at[:, pl.ds(at, height)],
                    out_ref.at[0, :, pl.ds(low, height)],
                    sems.at[n],
                )
            )
            copies[-1].start()
            at += height
        for copy in copies:
            copy.wait()

    return kernel


def gradient_kernel(
    pos_ref, start_ref, previous_ref, background_ref, near_ref, far_ref, edge_ref,
    out_ref, buffer, held, sems
):
    strip = out_ref.shape[2]

    def fill(source):
        def place(low, height, source_adj):
            here = slice(low, low + height)
            state = start_ref[:, HALO + low : HALO + low + height]
            buffer[:, here] = defect_weight * (state - source[:, here]) + source_adj

        cut = BLK + near_ref.shape[1]
        place(0, BLK, edge_ref[:, :BLK])
        place(BLK, near_ref.shape[1], near_ref[...])
        place(cut, far_ref.shape[1], far_ref[...])
        place(strip - BLK, BLK, edge_ref[:, BLK:])

    @pl.when(pos_ref[4] == 1)
    def _():
        copy = pltpu.make_async_copy(background_ref, held, sems.at[0])
        copy.start()
        copy.wait()
        fill(held)

    @pl.when(pos_ref[4] != 1)
    def _():
        fill(previous_ref)

    copy = pltpu.make_async_copy(buffer, out_ref.at[0], sems.at[1])
    copy.start()
    copy.wait()


def shifted(block, axis, distance):
    devices = range(lax.axis_size(axis))
    route = [(i - distance, i) for i in devices if i - distance in devices]
    return lax.ppermute(block, axis, route)


def local(states, background, obs_cells, obs_values, land_mask):
    strip, columns = states.shape[2], states.shape[3]
    rows = strip + 2 * HALO
    at_first = lax.axis_index("tm") == 0
    at_final = lax.axis_index("tm") == lax.axis_size("tm") - 1
    base = lax.axis_index("space") * strip - HALO
    odd = lax.axis_index("space") & 1
    pos = jnp.stack(
        [
            base,
            jnp.int32(strip) * lax.axis_size("space"),
            at_final.astype(jnp.int32),
            odd,
            at_first.astype(jnp.int32),
            ((lax.axis_index("tm") & (RING - 1) < 2) & (lax.axis_index("tm") >= RING)).astype(jnp.int32),
        ]
    ).astype(jnp.int32)
    f32 = jnp.float32

    def params(megabytes):
        return pltpu.CompilerParams(vmem_limit_bytes=megabytes * 1024 * 1024)

    def cost(us):
        return pl.CostEstimate(
            flops=int(us * 1.0e9), transcendentals=0, bytes_accessed=int(us * 3.0e6)
        )

    observed = obs_cells.shape[2]
    cut = near_blocks(strip // BLK) * BLK
    cross, pair, cells, values, near, far, count, total = pl.pallas_call(
        prepare_kernel,
        out_shape=(
            jax.ShapeDtypeStruct((4, HALO, columns), f32),
            jax.ShapeDtypeStruct((4, HALO, columns), f32),
            jax.ShapeDtypeStruct((NSTEP, observed), jnp.int32),
            jax.ShapeDtypeStruct((NSTEP, observed), f32),
            jax.ShapeDtypeStruct((3, cut, columns), f32),
            jax.ShapeDtypeStruct((3, strip - cut, columns), f32),
            jax.ShapeDtypeStruct((NSTEP, rows, columns), f32),
            jax.ShapeDtypeStruct((NSTEP, rows, columns), f32),
        ),
        in_specs=[smem()] + [hbm()] * 4,
        out_specs=(vmem(),) * 8,
        scratch_shapes=[
            pltpu.VMEM((2, HALO, columns), jnp.int32),
            pltpu.SemaphoreType.DMA((8,)),
        ],
        compiler_params=params(16),
        cost_estimate=cost(0.5),
        name="prepare",
    )(pos, *(off_chip(x) for x in (states, land_mask, obs_cells, obs_values)))
    cross, pair, near, far, pos, even = lax.optimization_barrier(
        (cross, pair, near, far, pos, odd == 0)
    )
    strips = lax.axis_size("space")
    inner = [(i, i ^ 1) for i in range(strips)]
    outer = [(i, j) for i in range(strips) for j in [((i + 1) ^ 1) - 1] if 0 <= j < strips]
    cross = lax.ppermute(cross, "space", outer)
    pair = lax.ppermute(pair, "space", inner)
    far = shifted(far, "tm", -1)
    near = shifted(near, "tm", -1)

    count, total, start, bits = pl.pallas_call(
        maps_kernel,
        out_shape=(
            jax.ShapeDtypeStruct((NSTEP, rows, columns), f32),
            jax.ShapeDtypeStruct((NSTEP, rows, columns), f32),
            jax.ShapeDtypeStruct((3, rows, columns), f32),
            jax.ShapeDtypeStruct((strip, columns), jnp.int32),
        ),
        in_specs=[smem(), vmem(), vmem(), hbm(), hbm(), vmem(), vmem()],
        out_specs=(vmem(),) * 4,
        input_output_aliases={5: 0, 6: 1},
        scratch_shapes=[pltpu.SemaphoreType.DMA((2,))],
        compiler_params=params(16),
        cost_estimate=cost(4),
        name="maps",
    )(pos, cells, values, off_chip(states), off_chip(land_mask), count, total)

    def advanced(early, start, *held):
        return pl.pallas_call(
            forward_kernel(early),
            out_shape=(
                jax.ShapeDtypeStruct((rows, columns), f32),
                jax.ShapeDtypeStruct((3, strip, columns), f32),
            )
            + (jax.ShapeDtypeStruct((3, rows, columns), f32),) * (NSTEP + 1),
            in_specs=[smem()] + [vmem()] * (4 + len(held)),
            out_specs=(vmem(),) * (NSTEP + 3),
            input_output_aliases={1: 2}
            | {5 + n: n if n < 2 else n + 1 for n in range(len(held))},
            compiler_params=params(24),
            cost_estimate=cost(0.01 if early else 2),
            name="forward_early" if early else "forward_late",
        )(pos, start, cross, pair, bits, *held)

    row = lax.broadcasted_iota(jnp.int32, (3, HALO, columns), 1)
    rim = jnp.where((row < HALO // 2) != even, cross[:3], pair[:3])
    land, ends, *path = advanced(True, start)
    rim, cross, pair, land, ends, path = lax.optimization_barrier(
        (rim, cross, pair, land, ends, path)
    )
    rim = shifted(rim, "tm", -1)
    land, ends, *path = advanced(False, path[0], land, ends, *path[1:])

    previous = shifted(ends, "tm", 1)

    def adjoint(part, height, *operands):
        work = jax.ShapeDtypeStruct((NSTEP, 3, rows, columns), f32)
        return pl.pallas_call(
            adjoint_kernel(part),
            out_shape=(jax.ShapeDtypeStruct((3, height, columns), f32),) * 2 + (work,),
            in_specs=[smem()] + [vmem()] * len(operands),
            out_specs=(vmem(),) * 3,
            input_output_aliases={} if part == "near" else {len(operands): 2},
            compiler_params=params(24),
            cost_estimate=cost({"near": 0.1, "far": 60, "edge": 0.5}[part]),
            name="adjoint_" + part,
        )(pos, *operands)

    shared = (land, count, total, *path)
    first, near_send, work = adjoint("near", cut - 2 * BLK, *shared, near)
    second, far_send, work = adjoint("far", strip - cut, *shared, far, work)
    outer, edge_send, work = adjoint("edge", 2 * BLK, *shared, rim, work)
    edge_sent = shifted(edge_send, "tm", -1)
    far_sent = shifted(far_send, "tm", -1)
    near_sent = shifted(near_send, "tm", -1)

    def settle(name, places, arrived, *held):
        height = arrived.shape[1]
        return pl.pallas_call(
            settle_kernel(places),
            out_shape=jax.ShapeDtypeStruct(states.shape, f32),
            in_specs=[smem()] + [vmem()] * 2 + [hbm()] * len(held),
            out_specs=hbm(),
            scratch_shapes=[
                pltpu.VMEM((3, height, columns), f32),
                pltpu.SemaphoreType.DMA((len(places),)),
            ],
            input_output_aliases={3: 0} if held else {},
            compiler_params=params(8),
            cost_estimate=cost(0.01),
            name="settle_" + name,
        )(pos, ends, arrived, *(off_chip(x) for x in held))

    gradient = pl.pallas_call(
        gradient_kernel,
        out_shape=jax.ShapeDtypeStruct(states.shape, f32),
        in_specs=[smem(), vmem(), vmem(), hbm(), vmem(), vmem(), vmem()],
        out_specs=hbm(),
        scratch_shapes=[
            pltpu.VMEM((3, strip, columns), f32),
            pltpu.VMEM((3, strip, columns), f32),
            pltpu.SemaphoreType.DMA((2,)),
        ],
        compiler_params=params(12),
        cost_estimate=cost(0.01),
        name="gradient",
    )(pos, path[0], previous, off_chip(background), first, second, outer)
    next_state = settle("near", [(BLK, cut - 2 * BLK)], near_sent)
    next_state = settle("far", [(cut - BLK, strip - cut)], far_sent, next_state)
    next_state = settle("edge", [(0, BLK), (strip - BLK, BLK)], edge_sent, next_state, gradient)
    return (gradient, next_state)


def solution(mesh):
    in_specs = (
        P("tm", None, "space", None),
        P(None, "space", None),
        P("tm", None, None),
        P("tm", None, None),
        P("space", None),
    )
    out_specs = (P("tm", None, "space", None), P("tm", None, "space", None))
    return jax.shard_map(local, mesh=mesh, in_specs=in_specs, out_specs=out_specs, check_vma=False)
```

```python
import jax
import jax.numpy as jnp
from jax import lax
from jax.experimental import pallas as pl
from jax.experimental.pallas import tpu as pltpu
from jax.sharding import PartitionSpec as P

NSTEP = 4
HALO = 8
BLK = 8
RING = 8

advect = 0.25
coriolis = 0.1
diffuse = 0.1
defect_weight = 2.0
obs_weight = 4.0
step_length = 0.1


def vmem():
    return pl.BlockSpec(memory_space=pltpu.VMEM)


def hbm():
    return pl.BlockSpec(memory_space=pltpu.HBM)


def off_chip(x):
    return pltpu.with_memory_space_constraint(x, pltpu.HBM)


def smem():
    return pl.BlockSpec(memory_space=pltpu.SMEM)


def east(x):
    return pltpu.roll(x, x.shape[1] - 1, axis=1)


def west(x):
    return pltpu.roll(x, 1, axis=1)


def below(x, after):
    first = lax.broadcasted_iota(jnp.int32, x.shape, 0) == 0
    return pltpu.roll(jnp.where(first, after, x), BLK - 1, axis=0)


def above(x, before):
    last = lax.broadcasted_iota(jnp.int32, x.shape, 0) == BLK - 1
    return pltpu.roll(jnp.where(last, before, x), 1, axis=0)


def fill_maps(pos_ref, cells_ref, values_ref, count_ref, total_ref):
    rows, columns = count_ref.shape[1:]
    observed = cells_ref.shape[1]
    shift = columns.bit_length() - 1
    assert columns == 1 << shift
    width = 256
    base = pos_ref[0]
    row_iota = lax.broadcasted_iota(jnp.int32, (rows, observed), 0)
    col_iota = lax.broadcasted_iota(jnp.int32, (width, observed), 0)
    for step in range(NSTEP):
        cells = cells_ref[step : step + 1, :]
        values = obs_weight * values_ref[step : step + 1, :]
        row = lax.shift_right_logical(cells, shift)
        col = cells - lax.shift_left(row, shift)
        inside = row_iota == row - base
        first = values.astype(jnp.bfloat16).astype(jnp.float32)
        rest = values - first
        second = rest.astype(jnp.bfloat16).astype(jnp.float32)
        third = rest - second
        zero = jnp.zeros((rows, observed), jnp.float32)
        parts = [
            jnp.where(inside, jnp.broadcast_to(part, (rows, observed)), zero).astype(jnp.bfloat16)
            for part in (first, second, third)
        ]
        picks = jnp.where(inside, jnp.float32(obs_weight), zero).astype(jnp.bfloat16)
        left = jnp.concatenate([picks] + parts, axis=0)
        for start in range(0, columns, width):
            hot = jnp.where(col_iota == col - start, jnp.float32(1), jnp.float32(0))
            hot = hot.astype(jnp.bfloat16)
            out = lax.dot_general(
                left, hot, (((1,), (1,)), ((), ())), preferred_element_type=jnp.float32
            )
            count_ref[step, :, start : start + width] = out[:rows]
            total_ref[step, :, start : start + width] = (
                out[rows : 2 * rows] + out[2 * rows : 3 * rows] + out[3 * rows :]
            )


def fetch(states_ref, mask_ref, start_ref, bits_ref, sems, first):
    strip = mask_ref.shape[0]
    return (
        pltpu.make_async_copy(
            states_ref.at[0], start_ref.at[:, pl.ds(HALO, strip)], sems.at[first]
        ),
        pltpu.make_async_copy(mask_ref, bits_ref, sems.at[first + 1]),
    )


def maps_kernel(*refs):
    pos_ref, cells_ref, values_ref, states_ref, mask_ref = refs[:5]
    count_ref, total_ref, start_ref, bits_ref, sems = refs[-5:]

    @pl.when(pos_ref[5] == 0)
    def _():
        copies = fetch(states_ref, mask_ref, start_ref, bits_ref, sems, 0)
        for copy in copies:
            copy.start()
        fill_maps(pos_ref, cells_ref, values_ref, count_ref, total_ref)
        for copy in copies:
            copy.wait()


def prepare_kernel(
    pos_ref, states_ref, mask_ref, cells_ref, values_ref,
    cross_ref, pair_ref, seen_ref, wanted_ref, near_ref, far_ref,
    count_ref, total_ref, start_ref, bits_ref, bits, sems
):
    strip = states_ref.shape[2]
    bottom = strip - HALO
    odd = pos_ref[3]
    copies = []
    for n, (out, at) in enumerate(((cross_ref, odd * bottom), (pair_ref, (1 - odd) * bottom))):
        at = pl.multiple_of(at, HALO)
        copies.append(
            pltpu.make_async_copy(mask_ref.at[pl.ds(at, HALO)], bits.at[n], sems.at[2 * n])
        )
        copies.append(
            pltpu.make_async_copy(
                states_ref.at[0, :, pl.ds(at, HALO)], out.at[pl.ds(0, 3)], sems.at[2 * n + 1]
            )
        )
    cut = near_ref.shape[1]
    copies.append(pltpu.make_async_copy(states_ref.at[0, :, pl.ds(0, cut)], near_ref, sems.at[6]))
    copies.append(
        pltpu.make_async_copy(states_ref.at[0, :, pl.ds(cut, strip - cut)], far_ref, sems.at[7])
    )
    copies.append(pltpu.make_async_copy(cells_ref.at[0], seen_ref, sems.at[4]))
    copies.append(pltpu.make_async_copy(values_ref.at[0], wanted_ref, sems.at[5]))
    for copy in copies:
        copy.start()
    for copy in copies:
        copy.wait()
    cross_ref[3] = bits[0].astype(jnp.float32)
    pair_ref[3] = bits[1].astype(jnp.float32)

    @pl.when(pos_ref[5] != 0)
    def _():
        later = fetch(states_ref, mask_ref, start_ref, bits_ref, sems, 8)
        for copy in later:
            copy.start()
        fill_maps(pos_ref, seen_ref, wanted_ref, count_ref, total_ref)
        for copy in later:
            copy.wait()


def forward(pos_ref, cross_ref, pair_ref, mask_ref, land_ref, ends_ref, path_ref):
    strip, columns = mask_ref.shape
    rows = strip + 2 * HALO
    blocks = rows // BLK
    base = pos_ref[0]
    grid_rows = pos_ref[1]
    odd = pos_ref[3] == 1
    up = jnp.where(odd, pair_ref[...], cross_ref[...])
    down = jnp.where(odd, cross_ref[...], pair_ref[...])
    path_ref[0][:, :HALO] = up[:3]
    path_ref[0][:, HALO + strip :] = down[:3]
    land_ref[:HALO] = up[3]
    land_ref[HALO : HALO + strip] = mask_ref[...].astype(jnp.float32)
    land_ref[HALO + strip :] = down[3]

    for step in range(NSTEP):
        for i in range(blocks):
            at = slice(i * BLK, (i + 1) * BLK)
            prior = slice(max(i - 1, 0) * BLK, (max(i - 1, 0) + 1) * BLK)
            follow = slice(min(i + 1, blocks - 1) * BLK, (min(i + 1, blocks - 1) + 1) * BLK)
            h, u, v = (path_ref[step][f, at] for f in range(3))
            h0, u0, v0 = (path_ref[step][f, prior] for f in range(3))
            h2, u2, v2 = (path_ref[step][f, follow] for f in range(3))
            hn, un, vn = below(h, h2), below(u, u2), below(v, v2)
            hs, us, vs = above(h, h0), above(u, u0), above(v, v0)
            land = land_ref[at]
            half = advect / 2.0
            dh = diffuse * h
            fx = half * ((1.0 + h) * u)
            gy = half * ((1.0 + hn) * vn - (1.0 + hs) * vs)
            keep = 1.0 - 4.0 * diffuse
            h_new = keep * h + diffuse * (hn + hs) - gy + east(dh - fx) + west(dh + fx)
            du = diffuse * u
            sx = half * h
            u_new = land * (
                keep * u + coriolis * v + diffuse * (un + us) + east(du - sx) + west(du + sx)
            )
            v_new = land * (
                keep * v
                - coriolis * u
                + diffuse * (vn + vs + east(v) + west(v))
                - half * (hn - hs)
            )
            number = base + i * BLK + lax.broadcasted_iota(jnp.int32, (BLK, columns), 0)
            inside = (number >= 0) & (number < grid_rows)
            h_new = jnp.where(inside, h_new, 0.0)
            path_ref[step + 1][0, at] = h_new
            path_ref[step + 1][1, at] = u_new
            path_ref[step + 1][2, at] = v_new
    ends_ref[...] = path_ref[NSTEP][:, HALO : HALO + strip]


def forward_kernel(early):
    def kernel(*refs):
        pos_ref, start_ref, cross_ref, pair_ref, mask_ref = refs[:5]
        land_ref, ends_ref, *path_ref = refs[-(NSTEP + 3) :]

        @pl.when(pos_ref[5] == (1 if early else 0))
        def _():
            forward(pos_ref, cross_ref, pair_ref, mask_ref, land_ref, ends_ref, path_ref)

    return kernel


def near_blocks(blocks):
    return blocks // 2 + 1


def adjoint_kernel(part):
    def kernel(*refs):
        pos_ref, land_ref, count_ref, total_ref, *path_ref = refs[: NSTEP + 5]
        ahead_ref = refs[NSTEP + 5]
        out_ref, send_ref, work = refs[-3:]
        rows, columns = land_ref.shape
        blocks = rows // BLK
        last = blocks - 2
        cut = near_blocks(last)
        base = pos_ref[0]
        grid_rows = pos_ref[1]
        weight = jnp.where(pos_ref[2] == 1, 0.0, defect_weight).astype(jnp.float32)
        half = advect / 2.0
        keep = 1.0 - 4.0 * diffuse
        if part == "near":
            first, inner, final = range(1, cut + 1), range(1, cut + 1), range(2, cut)
            low, high = 1, cut
        elif part == "far":
            first, inner, final = range(cut + 1, last + 1), range(cut, last + 1), range(cut, last)
            low, high = cut - 1, last
        else:
            first, inner, final = (0, last + 1), (0, 1, last, last + 1), (1, last)
            low, high = 0, last + 1

        def get(step, f, i):
            return work[step, f, i * BLK : (i + 1) * BLK]

        def put(step, i, lam):
            at = slice(i * BLK, (i + 1) * BLK)
            number = base + i * BLK + lax.broadcasted_iota(jnp.int32, (BLK, columns), 0)
            inside = (number >= 0) & (number < grid_rows)
            force = count_ref[step, at] * path_ref[step + 1][0, at] - total_ref[step, at]
            land = land_ref[at]
            work[step, 0, at] = jnp.where(inside, lam[0] + force, 0.0)
            work[step, 1, at] = land * lam[1]
            work[step, 2, at] = land * lam[2]

        for i in first:
            at = slice(i * BLK, (i + 1) * BLK)
            if part == "edge":
                ahead = [ahead_ref[f] for f in range(3)]
            else:
                here = slice((i - first[0]) * BLK, (i - first[0] + 1) * BLK)
                ahead = [ahead_ref[f, here] for f in range(3)]
            put(
                NSTEP - 1,
                i,
                [weight * (path_ref[NSTEP][f, at] - ahead[f]) for f in range(3)],
            )

        for step in reversed(range(NSTEP)):
            for n, i in enumerate(inner if step > 0 else final):
                at = slice(i * BLK, (i + 1) * BLK)
                before, after = max(i - 1, low), min(i + 1, high)
                a, b, c = (get(step, f, i) for f in range(3))
                a0, b0, c0 = (get(step, f, before) for f in range(3))
                a2, b2, c2 = (get(step, f, after) for f in range(3))
                an, bn, cn = below(a, a2), below(b, b2), below(c, c2)
                as_, bs, cs = above(a, a0), above(b, b0), above(c, c0)
                ae, aw = east(a), west(a)
                be, bw = east(b), west(b)
                ce, cw = east(c), west(c)
                h, u, v = (path_ref[step][f, at] for f in range(3))
                fx = half * (ae - aw)
                gy = half * (an - as_)
                depth = 1.0 + h
                lh = (
                    keep * a
                    + diffuse * (ae + aw + an + as_)
                    + u * fx
                    + v * gy
                    + half * (be - bw + cn - cs)
                )
                lu = depth * fx + keep * b - coriolis * c + diffuse * (be + bw + bn + bs)
                lv = depth * gy + keep * c + coriolis * b + diffuse * (ce + cw + cn + cs)
                if step > 0:
                    put(step - 1, i, (lh, lu, lv))
                else:
                    here = slice(n * BLK, (n + 1) * BLK)
                    for f, (lam, x) in enumerate(((lh, h), (lu, u), (lv, v))):
                        out_ref[f, here] = lam
                        send_ref[f, here] = (
                            1.0 - step_length * defect_weight
                        ) * x - step_length * lam

    return kernel


def settle_kernel(places):
    def kernel(*refs):
        pos_ref, ends_ref, got_ref = refs[:3]
        out_ref, buffer, sems = refs[-3:]
        share = jnp.where(pos_ref[2] == 1, 1.0, step_length * defect_weight).astype(jnp.float32)
        copies = []
        at = 0
        for n, (low, height) in enumerate(places):
            here = slice(at, at + height)
            buffer[:, here] = got_ref[:, here] + share * ends_ref[:, low : low + height]
            copies.append(
                pltpu.make_async_copy(
                    buffer.at[:, pl.ds(at, height)],
                    out_ref.at[0, :, pl.ds(low, height)],
                    sems.at[n],
                )
            )
            copies[-1].start()
            at += height
        for copy in copies:
            copy.wait()

    return kernel


def gradient_kernel(
    pos_ref, start_ref, previous_ref, background_ref, near_ref, far_ref, edge_ref,
    out_ref, buffer, held, sems
):
    strip = out_ref.shape[2]

    def fill(source):
        def place(low, height, source_adj):
            here = slice(low, low + height)
            state = start_ref[:, HALO + low : HALO + low + height]
            buffer[:, here] = defect_weight * (state - source[:, here]) + source_adj

        cut = BLK + near_ref.shape[1]
        place(0, BLK, edge_ref[:, :BLK])
        place(BLK, near_ref.shape[1], near_ref[...])
        place(cut, far_ref.shape[1], far_ref[...])
        place(strip - BLK, BLK, edge_ref[:, BLK:])

    @pl.when(pos_ref[4] == 1)
    def _():
        copy = pltpu.make_async_copy(background_ref, held, sems.at[0])
        copy.start()
        copy.wait()
        fill(held)

    @pl.when(pos_ref[4] != 1)
    def _():
        fill(previous_ref)

    copy = pltpu.make_async_copy(buffer, out_ref.at[0], sems.at[1])
    copy.start()
    copy.wait()


def shifted(block, axis, distance):
    devices = range(lax.axis_size(axis))
    route = [(i - distance, i) for i in devices if i - distance in devices]
    return lax.ppermute(block, axis, route)


def local(states, background, obs_cells, obs_values, land_mask):
    strip, columns = states.shape[2], states.shape[3]
    rows = strip + 2 * HALO
    at_first = lax.axis_index("tm") == 0
    at_final = lax.axis_index("tm") == lax.axis_size("tm") - 1
    base = lax.axis_index("space") * strip - HALO
    odd = lax.axis_index("space") & 1
    pos = jnp.stack(
        [
            base,
            jnp.int32(strip) * lax.axis_size("space"),
            at_final.astype(jnp.int32),
            odd,
            at_first.astype(jnp.int32),
            ((lax.axis_index("tm") & (RING - 1) < 3) & (lax.axis_index("tm") >= RING)).astype(jnp.int32),
        ]
    ).astype(jnp.int32)
    f32 = jnp.float32

    def params(megabytes):
        return pltpu.CompilerParams(vmem_limit_bytes=megabytes * 1024 * 1024)

    def cost(us):
        return pl.CostEstimate(
            flops=int(us * 1.0e9), transcendentals=0, bytes_accessed=int(us * 3.0e6)
        )

    observed = obs_cells.shape[2]
    cut = near_blocks(strip // BLK) * BLK
    map_shapes = (
        jax.ShapeDtypeStruct((NSTEP, rows, columns), f32),
        jax.ShapeDtypeStruct((NSTEP, rows, columns), f32),
        jax.ShapeDtypeStruct((3, rows, columns), f32),
        jax.ShapeDtypeStruct((strip, columns), jnp.int32),
    )
    cross, pair, cells, values, near, far, *maps = pl.pallas_call(
        prepare_kernel,
        out_shape=(
            jax.ShapeDtypeStruct((4, HALO, columns), f32),
            jax.ShapeDtypeStruct((4, HALO, columns), f32),
            jax.ShapeDtypeStruct((NSTEP, observed), jnp.int32),
            jax.ShapeDtypeStruct((NSTEP, observed), f32),
            jax.ShapeDtypeStruct((3, cut, columns), f32),
            jax.ShapeDtypeStruct((3, strip - cut, columns), f32),
        )
        + map_shapes,
        in_specs=[smem()] + [hbm()] * 4,
        out_specs=(vmem(),) * 10,
        scratch_shapes=[
            pltpu.VMEM((2, HALO, columns), jnp.int32),
            pltpu.SemaphoreType.DMA((10,)),
        ],
        compiler_params=params(16),
        cost_estimate=cost(0.5),
        name="prepare",
    )(pos, *(off_chip(x) for x in (states, land_mask, obs_cells, obs_values)))
    cross, pair, near, far, pos, even = lax.optimization_barrier(
        (cross, pair, near, far, pos, odd == 0)
    )
    strips = lax.axis_size("space")
    inner = [(i, i ^ 1) for i in range(strips)]
    outer = [(i, j) for i in range(strips) for j in [((i + 1) ^ 1) - 1] if 0 <= j < strips]
    cross = lax.ppermute(cross, "space", outer)
    pair = lax.ppermute(pair, "space", inner)
    far = shifted(far, "tm", -1)
    near = shifted(near, "tm", -1)

    count, total, start, bits = pl.pallas_call(
        maps_kernel,
        out_shape=map_shapes,
        in_specs=[smem(), vmem(), vmem(), hbm(), hbm()] + [vmem()] * 4,
        out_specs=(vmem(),) * 4,
        input_output_aliases={5: 0, 6: 1, 7: 2, 8: 3},
        scratch_shapes=[pltpu.SemaphoreType.DMA((2,))],
        compiler_params=params(16),
        cost_estimate=cost(4),
        name="maps",
    )(pos, cells, values, off_chip(states), off_chip(land_mask), *maps)

    def advanced(early, start, *held):
        return pl.pallas_call(
            forward_kernel(early),
            out_shape=(
                jax.ShapeDtypeStruct((rows, columns), f32),
                jax.ShapeDtypeStruct((3, strip, columns), f32),
            )
            + (jax.ShapeDtypeStruct((3, rows, columns), f32),) * (NSTEP + 1),
            in_specs=[smem()] + [vmem()] * (4 + len(held)),
            out_specs=(vmem(),) * (NSTEP + 3),
            input_output_aliases={1: 2}
            | {5 + n: n if n < 2 else n + 1 for n in range(len(held))},
            compiler_params=params(24),
            cost_estimate=cost(0.01 if early else 2),
            name="forward_early" if early else "forward_late",
        )(pos, start, cross, pair, bits, *held)

    row = lax.broadcasted_iota(jnp.int32, (3, HALO, columns), 1)
    rim = jnp.where((row < HALO // 2) != even, cross[:3], pair[:3])
    land, ends, *path = advanced(True, start)
    rim, cross, pair, land, ends, path = lax.optimization_barrier(
        (rim, cross, pair, land, ends, path)
    )
    rim = shifted(rim, "tm", -1)
    land, ends, *path = advanced(False, path[0], land, ends, *path[1:])

    previous = shifted(ends, "tm", 1)

    def adjoint(part, height, *operands):
        work = jax.ShapeDtypeStruct((NSTEP, 3, rows, columns), f32)
        return pl.pallas_call(
            adjoint_kernel(part),
            out_shape=(jax.ShapeDtypeStruct((3, height, columns), f32),) * 2 + (work,),
            in_specs=[smem()] + [vmem()] * len(operands),
            out_specs=(vmem(),) * 3,
            input_output_aliases={} if part == "near" else {len(operands): 2},
            compiler_params=params(24),
            cost_estimate=cost({"near": 0.1, "far": 60, "edge": 0.5}[part]),
            name="adjoint_" + part,
        )(pos, *operands)

    shared = (land, count, total, *path)
    first, near_send, work = adjoint("near", cut - 2 * BLK, *shared, near)
    second, far_send, work = adjoint("far", strip - cut, *shared, far, work)
    outer, edge_send, work = adjoint("edge", 2 * BLK, *shared, rim, work)
    edge_sent = shifted(edge_send, "tm", -1)
    far_sent = shifted(far_send, "tm", -1)
    near_sent = shifted(near_send, "tm", -1)

    def settle(name, places, arrived, *held):
        height = arrived.shape[1]
        return pl.pallas_call(
            settle_kernel(places),
            out_shape=jax.ShapeDtypeStruct(states.shape, f32),
            in_specs=[smem()] + [vmem()] * 2 + [hbm()] * len(held),
            out_specs=hbm(),
            scratch_shapes=[
                pltpu.VMEM((3, height, columns), f32),
                pltpu.SemaphoreType.DMA((len(places),)),
            ],
            input_output_aliases={3: 0} if held else {},
            compiler_params=params(8),
            cost_estimate=cost(0.01),
            name="settle_" + name,
        )(pos, ends, arrived, *(off_chip(x) for x in held))

    gradient = pl.pallas_call(
        gradient_kernel,
        out_shape=jax.ShapeDtypeStruct(states.shape, f32),
        in_specs=[smem(), vmem(), vmem(), hbm(), vmem(), vmem(), vmem()],
        out_specs=hbm(),
        scratch_shapes=[
            pltpu.VMEM((3, strip, columns), f32),
            pltpu.VMEM((3, strip, columns), f32),
            pltpu.SemaphoreType.DMA((2,)),
        ],
        compiler_params=params(12),
        cost_estimate=cost(0.01),
        name="gradient",
    )(pos, path[0], previous, off_chip(background), first, second, outer)
    next_state = settle("near", [(BLK, cut - 2 * BLK)], near_sent)
    next_state = settle("far", [(cut - BLK, strip - cut)], far_sent, next_state, gradient)
    next_state = settle("edge", [(0, BLK), (strip - BLK, BLK)], edge_sent, next_state)
    return (gradient, next_state)


def solution(mesh):
    in_specs = (
        P("tm", None, "space", None),
        P(None, "space", None),
        P("tm", None, None),
        P("tm", None, None),
        P("space", None),
    )
    out_specs = (P("tm", None, "space", None), P("tm", None, "space", None))
    return jax.shard_map(local, mesh=mesh, in_specs=in_specs, out_specs=out_specs, check_vma=False)
```

```python
import jax
import jax.numpy as jnp
from jax import lax
from jax.experimental import pallas as pl
from jax.experimental.pallas import tpu as pltpu
from jax.sharding import PartitionSpec as P

NSTEP = 4
HALO = 8
BLK = 8
RING = 8

advect = 0.25
coriolis = 0.1
diffuse = 0.1
defect_weight = 2.0
obs_weight = 4.0
step_length = 0.1


def vmem():
    return pl.BlockSpec(memory_space=pltpu.VMEM)


def hbm():
    return pl.BlockSpec(memory_space=pltpu.HBM)


def off_chip(x):
    return pltpu.with_memory_space_constraint(x, pltpu.HBM)


def smem():
    return pl.BlockSpec(memory_space=pltpu.SMEM)


def east(x):
    return pltpu.roll(x, x.shape[1] - 1, axis=1)


def west(x):
    return pltpu.roll(x, 1, axis=1)


def below(x, after):
    first = lax.broadcasted_iota(jnp.int32, x.shape, 0) == 0
    return pltpu.roll(jnp.where(first, after, x), BLK - 1, axis=0)


def above(x, before):
    last = lax.broadcasted_iota(jnp.int32, x.shape, 0) == BLK - 1
    return pltpu.roll(jnp.where(last, before, x), 1, axis=0)


def fill_maps(pos_ref, cells_ref, values_ref, count_ref, total_ref):
    rows, columns = count_ref.shape[1:]
    observed = cells_ref.shape[1]
    shift = columns.bit_length() - 1
    assert columns == 1 << shift
    width = 256
    base = pos_ref[0]
    row_iota = lax.broadcasted_iota(jnp.int32, (rows, observed), 0)
    col_iota = lax.broadcasted_iota(jnp.int32, (width, observed), 0)
    for step in range(NSTEP):
        cells = cells_ref[step : step + 1, :]
        values = obs_weight * values_ref[step : step + 1, :]
        row = lax.shift_right_logical(cells, shift)
        col = cells - lax.shift_left(row, shift)
        inside = row_iota == row - base
        first = values.astype(jnp.bfloat16).astype(jnp.float32)
        rest = values - first
        second = rest.astype(jnp.bfloat16).astype(jnp.float32)
        third = rest - second
        zero = jnp.zeros((rows, observed), jnp.float32)
        parts = [
            jnp.where(inside, jnp.broadcast_to(part, (rows, observed)), zero).astype(jnp.bfloat16)
            for part in (first, second, third)
        ]
        picks = jnp.where(inside, jnp.float32(obs_weight), zero).astype(jnp.bfloat16)
        left = jnp.concatenate([picks] + parts, axis=0)
        for start in range(0, columns, width):
            hot = jnp.where(col_iota == col - start, jnp.float32(1), jnp.float32(0))
            hot = hot.astype(jnp.bfloat16)
            out = lax.dot_general(
                left, hot, (((1,), (1,)), ((), ())), preferred_element_type=jnp.float32
            )
            count_ref[step, :, start : start + width] = out[:rows]
            total_ref[step, :, start : start + width] = (
                out[rows : 2 * rows] + out[2 * rows : 3 * rows] + out[3 * rows :]
            )


def fetch(states_ref, mask_ref, start_ref, bits_ref, sems, first):
    strip = mask_ref.shape[0]
    return (
        pltpu.make_async_copy(
            states_ref.at[0], start_ref.at[:, pl.ds(HALO, strip)], sems.at[first]
        ),
        pltpu.make_async_copy(mask_ref, bits_ref, sems.at[first + 1]),
    )


def prepare_kernel(
    pos_ref, states_ref, mask_ref, cells_ref, values_ref,
    cross_ref, pair_ref, seen_ref, wanted_ref, near_ref, far_ref,
    count_ref, total_ref, start_ref, bits_ref, bits, sems
):
    strip = states_ref.shape[2]
    bottom = strip - HALO
    odd = pos_ref[3]
    copies = []
    for n, (out, at) in enumerate(((cross_ref, odd * bottom), (pair_ref, (1 - odd) * bottom))):
        at = pl.multiple_of(at, HALO)
        copies.append(
            pltpu.make_async_copy(mask_ref.at[pl.ds(at, HALO)], bits.at[n], sems.at[2 * n])
        )
        copies.append(
            pltpu.make_async_copy(
                states_ref.at[0, :, pl.ds(at, HALO)], out.at[pl.ds(0, 3)], sems.at[2 * n + 1]
            )
        )
    cut = near_ref.shape[1]
    copies.append(pltpu.make_async_copy(states_ref.at[0, :, pl.ds(0, cut)], near_ref, sems.at[6]))
    copies.append(
        pltpu.make_async_copy(states_ref.at[0, :, pl.ds(cut, strip - cut)], far_ref, sems.at[7])
    )
    copies.append(pltpu.make_async_copy(cells_ref.at[0], seen_ref, sems.at[4]))
    copies.append(pltpu.make_async_copy(values_ref.at[0], wanted_ref, sems.at[5]))
    for copy in copies:
        copy.start()
    for copy in copies:
        copy.wait()
    cross_ref[3] = bits[0].astype(jnp.float32)
    pair_ref[3] = bits[1].astype(jnp.float32)

    @pl.when(pos_ref[5] != 0)
    def _():
        later = fetch(states_ref, mask_ref, start_ref, bits_ref, sems, 8)
        for copy in later:
            copy.start()
        fill_maps(pos_ref, seen_ref, wanted_ref, count_ref, total_ref)
        for copy in later:
            copy.wait()


def forward(pos_ref, cross_ref, pair_ref, mask_ref, land_ref, ends_ref, path_ref):
    strip, columns = mask_ref.shape
    rows = strip + 2 * HALO
    blocks = rows // BLK
    base = pos_ref[0]
    grid_rows = pos_ref[1]
    odd = pos_ref[3] == 1
    up = jnp.where(odd, pair_ref[...], cross_ref[...])
    down = jnp.where(odd, cross_ref[...], pair_ref[...])
    path_ref[0][:, :HALO] = up[:3]
    path_ref[0][:, HALO + strip :] = down[:3]
    land_ref[:HALO] = up[3]
    land_ref[HALO : HALO + strip] = mask_ref[...].astype(jnp.float32)
    land_ref[HALO + strip :] = down[3]

    for step in range(NSTEP):
        for i in range(blocks):
            at = slice(i * BLK, (i + 1) * BLK)
            prior = slice(max(i - 1, 0) * BLK, (max(i - 1, 0) + 1) * BLK)
            follow = slice(min(i + 1, blocks - 1) * BLK, (min(i + 1, blocks - 1) + 1) * BLK)
            h, u, v = (path_ref[step][f, at] for f in range(3))
            h0, u0, v0 = (path_ref[step][f, prior] for f in range(3))
            h2, u2, v2 = (path_ref[step][f, follow] for f in range(3))
            hn, un, vn = below(h, h2), below(u, u2), below(v, v2)
            hs, us, vs = above(h, h0), above(u, u0), above(v, v0)
            land = land_ref[at]
            half = advect / 2.0
            dh = diffuse * h
            fx = half * ((1.0 + h) * u)
            gy = half * ((1.0 + hn) * vn - (1.0 + hs) * vs)
            keep = 1.0 - 4.0 * diffuse
            h_new = keep * h + diffuse * (hn + hs) - gy + east(dh - fx) + west(dh + fx)
            du = diffuse * u
            sx = half * h
            u_new = land * (
                keep * u + coriolis * v + diffuse * (un + us) + east(du - sx) + west(du + sx)
            )
            v_new = land * (
                keep * v
                - coriolis * u
                + diffuse * (vn + vs + east(v) + west(v))
                - half * (hn - hs)
            )
            number = base + i * BLK + lax.broadcasted_iota(jnp.int32, (BLK, columns), 0)
            inside = (number >= 0) & (number < grid_rows)
            h_new = jnp.where(inside, h_new, 0.0)
            path_ref[step + 1][0, at] = h_new
            path_ref[step + 1][1, at] = u_new
            path_ref[step + 1][2, at] = v_new
    ends_ref[...] = path_ref[NSTEP][:, HALO : HALO + strip]


def early_kernel(pos_ref, start_ref, cross_ref, pair_ref, bits_ref, land_ref, ends_ref, *path_ref):
    @pl.when(pos_ref[5] != 0)
    def _():
        forward(pos_ref, cross_ref, pair_ref, bits_ref, land_ref, ends_ref, path_ref)


def late_kernel(*refs):
    pos_ref, cells_ref, values_ref, states_ref, mask_ref, cross_ref, pair_ref = refs[:7]
    count_ref, total_ref, bits_ref, land_ref, ends_ref, *path_ref = refs[-(NSTEP + 7) : -1]
    sems = refs[-1]

    @pl.when(pos_ref[5] == 0)
    def _():
        copies = fetch(states_ref, mask_ref, path_ref[0], bits_ref, sems, 0)
        for copy in copies:
            copy.start()
        fill_maps(pos_ref, cells_ref, values_ref, count_ref, total_ref)
        for copy in copies:
            copy.wait()
        forward(pos_ref, cross_ref, pair_ref, bits_ref, land_ref, ends_ref, path_ref)


def near_blocks(blocks):
    return blocks // 2 + 1


def adjoint_kernel(part):
    def kernel(*refs):
        pos_ref, land_ref, count_ref, total_ref, *path_ref = refs[: NSTEP + 5]
        ahead_ref = refs[NSTEP + 5]
        out_ref, send_ref, work = refs[-3:]
        rows, columns = land_ref.shape
        blocks = rows // BLK
        last = blocks - 2
        cut = near_blocks(last)
        base = pos_ref[0]
        grid_rows = pos_ref[1]
        weight = jnp.where(pos_ref[2] == 1, 0.0, defect_weight).astype(jnp.float32)
        half = advect / 2.0
        keep = 1.0 - 4.0 * diffuse
        if part == "near":
            first, inner, final = range(1, cut + 1), range(1, cut + 1), range(2, cut)
            low, high = 1, cut
        elif part == "far":
            first, inner, final = range(cut + 1, last + 1), range(cut, last + 1), range(cut, last)
            low, high = cut - 1, last
        else:
            first, inner, final = (0, last + 1), (0, 1, last, last + 1), (1, last)
            low, high = 0, last + 1

        def get(step, f, i):
            return work[step, f, i * BLK : (i + 1) * BLK]

        def put(step, i, lam):
            at = slice(i * BLK, (i + 1) * BLK)
            number = base + i * BLK + lax.broadcasted_iota(jnp.int32, (BLK, columns), 0)
            inside = (number >= 0) & (number < grid_rows)
            force = count_ref[step, at] * path_ref[step + 1][0, at] - total_ref[step, at]
            land = land_ref[at]
            work[step, 0, at] = jnp.where(inside, lam[0] + force, 0.0)
            work[step, 1, at] = land * lam[1]
            work[step, 2, at] = land * lam[2]

        for i in first:
            at = slice(i * BLK, (i + 1) * BLK)
            if part == "edge":
                ahead = [ahead_ref[f] for f in range(3)]
            else:
                here = slice((i - first[0]) * BLK, (i - first[0] + 1) * BLK)
                ahead = [ahead_ref[f, here] for f in range(3)]
            put(
                NSTEP - 1,
                i,
                [weight * (path_ref[NSTEP][f, at] - ahead[f]) for f in range(3)],
            )

        for step in reversed(range(NSTEP)):
            for n, i in enumerate(inner if step > 0 else final):
                at = slice(i * BLK, (i + 1) * BLK)
                before, after = max(i - 1, low), min(i + 1, high)
                a, b, c = (get(step, f, i) for f in range(3))
                a0, b0, c0 = (get(step, f, before) for f in range(3))
                a2, b2, c2 = (get(step, f, after) for f in range(3))
                an, bn, cn = below(a, a2), below(b, b2), below(c, c2)
                as_, bs, cs = above(a, a0), above(b, b0), above(c, c0)
                ae, aw = east(a), west(a)
                be, bw = east(b), west(b)
                ce, cw = east(c), west(c)
                h, u, v = (path_ref[step][f, at] for f in range(3))
                fx = half * (ae - aw)
                gy = half * (an - as_)
                depth = 1.0 + h
                lh = (
                    keep * a
                    + diffuse * (ae + aw + an + as_)
                    + u * fx
                    + v * gy
                    + half * (be - bw + cn - cs)
                )
                lu = depth * fx + keep * b - coriolis * c + diffuse * (be + bw + bn + bs)
                lv = depth * gy + keep * c + coriolis * b + diffuse * (ce + cw + cn + cs)
                if step > 0:
                    put(step - 1, i, (lh, lu, lv))
                else:
                    here = slice(n * BLK, (n + 1) * BLK)
                    for f, (lam, x) in enumerate(((lh, h), (lu, u), (lv, v))):
                        out_ref[f, here] = lam
                        send_ref[f, here] = (
                            1.0 - step_length * defect_weight
                        ) * x - step_length * lam

    return kernel


def settle_kernel(places):
    def kernel(*refs):
        pos_ref, ends_ref, got_ref = refs[:3]
        out_ref, buffer, sems = refs[-3:]
        share = jnp.where(pos_ref[2] == 1, 1.0, step_length * defect_weight).astype(jnp.float32)
        copies = []
        at = 0
        for n, (low, height) in enumerate(places):
            here = slice(at, at + height)
            buffer[:, here] = got_ref[:, here] + share * ends_ref[:, low : low + height]
            copies.append(
                pltpu.make_async_copy(
                    buffer.at[:, pl.ds(at, height)],
                    out_ref.at[0, :, pl.ds(low, height)],
                    sems.at[n],
                )
            )
            copies[-1].start()
            at += height
        for copy in copies:
            copy.wait()

    return kernel


def gradient_kernel(
    pos_ref, start_ref, previous_ref, background_ref, near_ref, far_ref, edge_ref,
    out_ref, buffer, held, sems
):
    strip = out_ref.shape[2]

    def fill(source):
        def place(low, height, source_adj):
            here = slice(low, low + height)
            state = start_ref[:, HALO + low : HALO + low + height]
            buffer[:, here] = defect_weight * (state - source[:, here]) + source_adj

        cut = BLK + near_ref.shape[1]
        place(0, BLK, edge_ref[:, :BLK])
        place(BLK, near_ref.shape[1], near_ref[...])
        place(cut, far_ref.shape[1], far_ref[...])
        place(strip - BLK, BLK, edge_ref[:, BLK:])

    @pl.when(pos_ref[4] == 1)
    def _():
        copy = pltpu.make_async_copy(background_ref, held, sems.at[0])
        copy.start()
        copy.wait()
        fill(held)

    @pl.when(pos_ref[4] != 1)
    def _():
        fill(previous_ref)

    copy = pltpu.make_async_copy(buffer, out_ref.at[0], sems.at[1])
    copy.start()
    copy.wait()


def shifted(block, axis, distance):
    devices = range(lax.axis_size(axis))
    route = [(i - distance, i) for i in devices if i - distance in devices]
    return lax.ppermute(block, axis, route)


def local(states, background, obs_cells, obs_values, land_mask):
    strip, columns = states.shape[2], states.shape[3]
    rows = strip + 2 * HALO
    at_first = lax.axis_index("tm") == 0
    at_final = lax.axis_index("tm") == lax.axis_size("tm") - 1
    base = lax.axis_index("space") * strip - HALO
    odd = lax.axis_index("space") & 1
    pos = jnp.stack(
        [
            base,
            jnp.int32(strip) * lax.axis_size("space"),
            at_final.astype(jnp.int32),
            odd,
            at_first.astype(jnp.int32),
            ((lax.axis_index("tm") & (RING - 1) < 3) & (lax.axis_index("tm") >= RING)).astype(jnp.int32),
        ]
    ).astype(jnp.int32)
    f32 = jnp.float32

    def params(megabytes):
        return pltpu.CompilerParams(vmem_limit_bytes=megabytes * 1024 * 1024)

    def cost(us):
        return pl.CostEstimate(
            flops=int(us * 1.0e9), transcendentals=0, bytes_accessed=int(us * 3.0e6)
        )

    observed = obs_cells.shape[2]
    cut = near_blocks(strip // BLK) * BLK
    map_shapes = (
        jax.ShapeDtypeStruct((NSTEP, rows, columns), f32),
        jax.ShapeDtypeStruct((NSTEP, rows, columns), f32),
        jax.ShapeDtypeStruct((3, rows, columns), f32),
        jax.ShapeDtypeStruct((strip, columns), jnp.int32),
    )
    cross, pair, cells, values, near, far, *maps = pl.pallas_call(
        prepare_kernel,
        out_shape=(
            jax.ShapeDtypeStruct((4, HALO, columns), f32),
            jax.ShapeDtypeStruct((4, HALO, columns), f32),
            jax.ShapeDtypeStruct((NSTEP, observed), jnp.int32),
            jax.ShapeDtypeStruct((NSTEP, observed), f32),
            jax.ShapeDtypeStruct((3, cut, columns), f32),
            jax.ShapeDtypeStruct((3, strip - cut, columns), f32),
        )
        + map_shapes,
        in_specs=[smem()] + [hbm()] * 4,
        out_specs=(vmem(),) * 10,
        scratch_shapes=[
            pltpu.VMEM((2, HALO, columns), jnp.int32),
            pltpu.SemaphoreType.DMA((10,)),
        ],
        compiler_params=params(16),
        cost_estimate=cost(0.5),
        name="prepare",
    )(pos, *(off_chip(x) for x in (states, land_mask, obs_cells, obs_values)))
    cross, pair, near, far, pos, even = lax.optimization_barrier(
        (cross, pair, near, far, pos, odd == 0)
    )
    strips = lax.axis_size("space")
    inner = [(i, i ^ 1) for i in range(strips)]
    outer = [(i, j) for i in range(strips) for j in [((i + 1) ^ 1) - 1] if 0 <= j < strips]
    cross = lax.ppermute(cross, "space", outer)
    pair = lax.ppermute(pair, "space", inner)
    far = shifted(far, "tm", -1)
    near = shifted(near, "tm", -1)

    count, total, start, bits = maps
    step_shapes = (
        jax.ShapeDtypeStruct((rows, columns), f32),
        jax.ShapeDtypeStruct((3, strip, columns), f32),
    ) + (jax.ShapeDtypeStruct((3, rows, columns), f32),) * (NSTEP + 1)
    row = lax.broadcasted_iota(jnp.int32, (3, HALO, columns), 1)
    rim = jnp.where((row < HALO // 2) != even, cross[:3], pair[:3])
    steps = pl.pallas_call(
        early_kernel,
        out_shape=step_shapes,
        in_specs=[smem()] + [vmem()] * 4,
        out_specs=(vmem(),) * len(step_shapes),
        input_output_aliases={1: 2},
        compiler_params=params(24),
        cost_estimate=cost(0.01),
        name="early",
    )(pos, start, cross, pair, bits)
    rim, cross, pair, steps = lax.optimization_barrier((rim, cross, pair, steps))
    rim = shifted(rim, "tm", -1)
    held = (count, total, bits, *steps)
    count, total, bits, land, ends, *path = pl.pallas_call(
        late_kernel,
        out_shape=(map_shapes[0], map_shapes[1], map_shapes[3]) + step_shapes,
        in_specs=[smem(), vmem(), vmem(), hbm(), hbm(), vmem(), vmem()] + [vmem()] * len(held),
        out_specs=(vmem(),) * len(held),
        input_output_aliases={7 + n: n for n in range(len(held))},
        scratch_shapes=[pltpu.SemaphoreType.DMA((2,))],
        compiler_params=params(28),
        cost_estimate=cost(6),
        name="late",
    )(pos, cells, values, off_chip(states), off_chip(land_mask), cross, pair, *held)

    previous = shifted(ends, "tm", 1)

    def adjoint(part, height, *operands):
        work = jax.ShapeDtypeStruct((NSTEP, 3, rows, columns), f32)
        return pl.pallas_call(
            adjoint_kernel(part),
            out_shape=(jax.ShapeDtypeStruct((3, height, columns), f32),) * 2 + (work,),
            in_specs=[smem()] + [vmem()] * len(operands),
            out_specs=(vmem(),) * 3,
            input_output_aliases={} if part == "near" else {len(operands): 2},
            compiler_params=params(24),
            cost_estimate=cost({"near": 0.1, "far": 60, "edge": 0.5}[part]),
            name="adjoint_" + part,
        )(pos, *operands)

    shared = (land, count, total, *path)
    first, near_send, work = adjoint("near", cut - 2 * BLK, *shared, near)
    second, far_send, work = adjoint("far", strip - cut, *shared, far, work)
    outer, edge_send, work = adjoint("edge", 2 * BLK, *shared, rim, work)
    edge_sent = shifted(edge_send, "tm", -1)
    far_sent = shifted(far_send, "tm", -1)
    near_sent = shifted(near_send, "tm", -1)

    def settle(name, places, arrived, *held):
        height = arrived.shape[1]
        return pl.pallas_call(
            settle_kernel(places),
            out_shape=jax.ShapeDtypeStruct(states.shape, f32),
            in_specs=[smem()] + [vmem()] * 2 + [hbm()] * len(held),
            out_specs=hbm(),
            scratch_shapes=[
                pltpu.VMEM((3, height, columns), f32),
                pltpu.SemaphoreType.DMA((len(places),)),
            ],
            input_output_aliases={3: 0} if held else {},
            compiler_params=params(8),
            cost_estimate=cost(0.01),
            name="settle_" + name,
        )(pos, ends, arrived, *(off_chip(x) for x in held))

    gradient = pl.pallas_call(
        gradient_kernel,
        out_shape=jax.ShapeDtypeStruct(states.shape, f32),
        in_specs=[smem(), vmem(), vmem(), hbm(), vmem(), vmem(), vmem()],
        out_specs=hbm(),
        scratch_shapes=[
            pltpu.VMEM((3, strip, columns), f32),
            pltpu.VMEM((3, strip, columns), f32),
            pltpu.SemaphoreType.DMA((2,)),
        ],
        compiler_params=params(12),
        cost_estimate=cost(0.01),
        name="gradient",
    )(pos, path[0], previous, off_chip(background), first, second, outer)
    next_state = settle("near", [(BLK, cut - 2 * BLK)], near_sent)
    next_state = settle("far", [(cut - BLK, strip - cut)], far_sent, next_state, gradient)
    next_state = settle("edge", [(0, BLK), (strip - BLK, BLK)], edge_sent, next_state)
    return (gradient, next_state)


def solution(mesh):
    in_specs = (
        P("tm", None, "space", None),
        P(None, "space", None),
        P("tm", None, None),
        P("tm", None, None),
        P("space", None),
    )
    out_specs = (P("tm", None, "space", None), P("tm", None, "space", None))
    return jax.shard_map(local, mesh=mesh, in_specs=in_specs, out_specs=out_specs, check_vma=False)
```

```python
import jax
import jax.numpy as jnp
from jax import lax
from jax.experimental import pallas as pl
from jax.experimental.pallas import tpu as pltpu
from jax.sharding import PartitionSpec as P

NSTEP = 4
HALO = 8
BLK = 8
RING = 8

advect = 0.25
coriolis = 0.1
diffuse = 0.1
defect_weight = 2.0
obs_weight = 4.0
step_length = 0.1


def vmem():
    return pl.BlockSpec(memory_space=pltpu.VMEM)


def hbm():
    return pl.BlockSpec(memory_space=pltpu.HBM)


def off_chip(x):
    return pltpu.with_memory_space_constraint(x, pltpu.HBM)


def smem():
    return pl.BlockSpec(memory_space=pltpu.SMEM)


def east(x):
    return pltpu.roll(x, x.shape[1] - 1, axis=1)


def west(x):
    return pltpu.roll(x, 1, axis=1)


def below(x, after):
    first = lax.broadcasted_iota(jnp.int32, x.shape, 0) == 0
    return pltpu.roll(jnp.where(first, after, x), BLK - 1, axis=0)


def above(x, before):
    last = lax.broadcasted_iota(jnp.int32, x.shape, 0) == BLK - 1
    return pltpu.roll(jnp.where(last, before, x), 1, axis=0)


def within(base, grid_rows, block, columns):
    number = base + block * BLK + lax.broadcasted_iota(jnp.int32, (BLK, columns), 0)
    return (number >= 0) & (number < grid_rows)


def fill_maps(pos_ref, cells_ref, values_ref, count_ref, total_ref):
    rows, columns = count_ref.shape[1:]
    observed = cells_ref.shape[1]
    shift = columns.bit_length() - 1
    assert columns == 1 << shift
    width = 256
    base = pos_ref[0]
    row_iota = lax.broadcasted_iota(jnp.int32, (rows, observed), 0)
    col_iota = lax.broadcasted_iota(jnp.int32, (width, observed), 0)
    for step in range(NSTEP):
        cells = cells_ref[step : step + 1, :]
        values = obs_weight * values_ref[step : step + 1, :]
        row = lax.shift_right_logical(cells, shift)
        col = cells - lax.shift_left(row, shift)
        inside = row_iota == row - base
        first = values.astype(jnp.bfloat16).astype(jnp.float32)
        rest = values - first
        second = rest.astype(jnp.bfloat16).astype(jnp.float32)
        third = rest - second
        zero = jnp.zeros((rows, observed), jnp.float32)
        parts = [
            jnp.where(inside, jnp.broadcast_to(part, (rows, observed)), zero).astype(jnp.bfloat16)
            for part in (first, second, third)
        ]
        picks = jnp.where(inside, jnp.float32(obs_weight), zero).astype(jnp.bfloat16)
        left = jnp.concatenate([picks] + parts, axis=0)
        for start in range(0, columns, width):
            hot = jnp.where(col_iota == col - start, jnp.float32(1), jnp.float32(0))
            hot = hot.astype(jnp.bfloat16)
            out = lax.dot_general(
                left, hot, (((1,), (1,)), ((), ())), preferred_element_type=jnp.float32
            )
            count_ref[step, :, start : start + width] = out[:rows]
            total_ref[step, :, start : start + width] = (
                out[rows : 2 * rows] + out[2 * rows : 3 * rows] + out[3 * rows :]
            )


def fetch(states_ref, mask_ref, start_ref, bits_ref, sems, first):
    strip = mask_ref.shape[0]
    return (
        pltpu.make_async_copy(
            states_ref.at[0], start_ref.at[:, pl.ds(HALO, strip)], sems.at[first]
        ),
        pltpu.make_async_copy(mask_ref, bits_ref, sems.at[first + 1]),
    )


def prepare_kernel(
    pos_ref, states_ref, mask_ref, cells_ref, values_ref,
    cross_ref, pair_ref, seen_ref, wanted_ref, near_ref, far_ref,
    count_ref, total_ref, start_ref, bits_ref, bits, sems
):
    strip = states_ref.shape[2]
    bottom = strip - HALO
    odd = pos_ref[3]
    copies = []
    for n, (out, at) in enumerate(((cross_ref, odd * bottom), (pair_ref, (1 - odd) * bottom))):
        at = pl.multiple_of(at, HALO)
        copies.append(
            pltpu.make_async_copy(mask_ref.at[pl.ds(at, HALO)], bits.at[n], sems.at[2 * n])
        )
        copies.append(
            pltpu.make_async_copy(
                states_ref.at[0, :, pl.ds(at, HALO)], out.at[pl.ds(0, 3)], sems.at[2 * n + 1]
            )
        )
    cut = near_ref.shape[1]
    copies.append(pltpu.make_async_copy(states_ref.at[0, :, pl.ds(0, cut)], near_ref, sems.at[6]))
    copies.append(
        pltpu.make_async_copy(states_ref.at[0, :, pl.ds(cut, strip - cut)], far_ref, sems.at[7])
    )
    copies.append(pltpu.make_async_copy(cells_ref.at[0], seen_ref, sems.at[4]))
    copies.append(pltpu.make_async_copy(values_ref.at[0], wanted_ref, sems.at[5]))
    for copy in copies:
        copy.start()
    for copy in copies:
        copy.wait()
    cross_ref[3] = bits[0].astype(jnp.float32)
    pair_ref[3] = bits[1].astype(jnp.float32)

    @pl.when(pos_ref[5] != 0)
    def _():
        later = fetch(states_ref, mask_ref, start_ref, bits_ref, sems, 8)
        for copy in later:
            copy.start()
        fill_maps(pos_ref, seen_ref, wanted_ref, count_ref, total_ref)
        for copy in later:
            copy.wait()


def forward(pos_ref, cross_ref, pair_ref, mask_ref, land_ref, ends_ref, path_ref):
    strip, columns = mask_ref.shape
    rows = strip + 2 * HALO
    blocks = rows // BLK
    base = pos_ref[0]
    grid_rows = pos_ref[1]
    odd = pos_ref[3] == 1
    up = jnp.where(odd, pair_ref[...], cross_ref[...])
    down = jnp.where(odd, cross_ref[...], pair_ref[...])
    path_ref[0][:, :HALO] = up[:3]
    path_ref[0][:, HALO + strip :] = down[:3]
    land_ref[:HALO] = up[3]
    land_ref[HALO : HALO + strip] = mask_ref[...].astype(jnp.float32)
    land_ref[HALO + strip :] = down[3]

    for step in range(NSTEP):
        for i in range(blocks):
            at = slice(i * BLK, (i + 1) * BLK)
            prior = slice(max(i - 1, 0) * BLK, (max(i - 1, 0) + 1) * BLK)
            follow = slice(min(i + 1, blocks - 1) * BLK, (min(i + 1, blocks - 1) + 1) * BLK)
            h, u, v = (path_ref[step][f, at] for f in range(3))
            h0, u0, v0 = (path_ref[step][f, prior] for f in range(3))
            h2, u2, v2 = (path_ref[step][f, follow] for f in range(3))
            hn, un, vn = below(h, h2), below(u, u2), below(v, v2)
            hs, us, vs = above(h, h0), above(u, u0), above(v, v0)
            land = land_ref[at]
            half = advect / 2.0
            dh = diffuse * h
            fx = half * ((1.0 + h) * u)
            gy = half * ((1.0 + hn) * vn - (1.0 + hs) * vs)
            keep = 1.0 - 4.0 * diffuse
            h_new = keep * h + diffuse * (hn + hs) - gy + east(dh - fx) + west(dh + fx)
            du = diffuse * u
            sx = half * h
            u_new = land * (
                keep * u + coriolis * v + diffuse * (un + us) + east(du - sx) + west(du + sx)
            )
            v_new = land * (
                keep * v
                - coriolis * u
                + diffuse * (vn + vs + east(v) + west(v))
                - half * (hn - hs)
            )
            if i in (0, blocks - 1):
                h_new = jnp.where(within(base, grid_rows, i, columns), h_new, 0.0)
            path_ref[step + 1][0, at] = h_new
            path_ref[step + 1][1, at] = u_new
            path_ref[step + 1][2, at] = v_new
    ends_ref[...] = path_ref[NSTEP][:, HALO : HALO + strip]


def early_kernel(pos_ref, start_ref, cross_ref, pair_ref, bits_ref, land_ref, ends_ref, *path_ref):
    @pl.when(pos_ref[5] != 0)
    def _():
        forward(pos_ref, cross_ref, pair_ref, bits_ref, land_ref, ends_ref, path_ref)


def late_kernel(*refs):
    pos_ref, cells_ref, values_ref, states_ref, mask_ref, cross_ref, pair_ref = refs[:7]
    count_ref, total_ref, bits_ref, land_ref, ends_ref, *path_ref = refs[-(NSTEP + 7) : -1]
    sems = refs[-1]

    @pl.when(pos_ref[5] == 0)
    def _():
        copies = fetch(states_ref, mask_ref, path_ref[0], bits_ref, sems, 0)
        for copy in copies:
            copy.start()
        fill_maps(pos_ref, cells_ref, values_ref, count_ref, total_ref)
        for copy in copies:
            copy.wait()
        forward(pos_ref, cross_ref, pair_ref, bits_ref, land_ref, ends_ref, path_ref)


def near_blocks(blocks):
    return blocks // 2 + 1


def adjoint_kernel(part):
    def kernel(*refs):
        pos_ref, land_ref, count_ref, total_ref, *path_ref = refs[: NSTEP + 5]
        ahead_ref = refs[NSTEP + 5]
        out_ref, send_ref, work = refs[-3:]
        rows, columns = land_ref.shape
        blocks = rows // BLK
        last = blocks - 2
        cut = near_blocks(last)
        base = pos_ref[0]
        grid_rows = pos_ref[1]
        weight = jnp.where(pos_ref[2] == 1, 0.0, defect_weight).astype(jnp.float32)
        half = advect / 2.0
        keep = 1.0 - 4.0 * diffuse
        if part == "near":
            first, inner, final = range(1, cut + 1), range(1, cut + 1), range(2, cut)
            low, high = 1, cut
        elif part == "far":
            first, inner, final = range(cut + 1, last + 1), range(cut, last + 1), range(cut, last)
            low, high = cut - 1, last
        else:
            first, inner, final = (0, last + 1), (0, 1, last, last + 1), (1, last)
            low, high = 0, last + 1

        def get(step, f, i):
            return work[step, f, i * BLK : (i + 1) * BLK]

        def put(step, i, lam):
            at = slice(i * BLK, (i + 1) * BLK)
            force = count_ref[step, at] * path_ref[step + 1][0, at] - total_ref[step, at]
            land = land_ref[at]
            height = lam[0] + force
            if i in (0, blocks - 1):
                height = jnp.where(within(base, grid_rows, i, columns), height, 0.0)
            work[step, 0, at] = height
            work[step, 1, at] = land * lam[1]
            work[step, 2, at] = land * lam[2]

        for i in first:
            at = slice(i * BLK, (i + 1) * BLK)
            if part == "edge":
                ahead = [ahead_ref[f] for f in range(3)]
            else:
                here = slice((i - first[0]) * BLK, (i - first[0] + 1) * BLK)
                ahead = [ahead_ref[f, here] for f in range(3)]
            put(
                NSTEP - 1,
                i,
                [weight * (path_ref[NSTEP][f, at] - ahead[f]) for f in range(3)],
            )

        for step in reversed(range(NSTEP)):
            for n, i in enumerate(inner if step > 0 else final):
                at = slice(i * BLK, (i + 1) * BLK)
                before, after = max(i - 1, low), min(i + 1, high)
                a, b, c = (get(step, f, i) for f in range(3))
                a0, b0, c0 = (get(step, f, before) for f in range(3))
                a2, b2, c2 = (get(step, f, after) for f in range(3))
                an, bn, cn = below(a, a2), below(b, b2), below(c, c2)
                as_, bs, cs = above(a, a0), above(b, b0), above(c, c0)
                ae, aw = east(a), west(a)
                be, bw = east(b), west(b)
                ce, cw = east(c), west(c)
                h, u, v = (path_ref[step][f, at] for f in range(3))
                fx = half * (ae - aw)
                gy = half * (an - as_)
                depth = 1.0 + h
                lh = (
                    keep * a
                    + diffuse * (ae + aw + an + as_)
                    + u * fx
                    + v * gy
                    + half * (be - bw + cn - cs)
                )
                lu = depth * fx + keep * b - coriolis * c + diffuse * (be + bw + bn + bs)
                lv = depth * gy + keep * c + coriolis * b + diffuse * (ce + cw + cn + cs)
                if step > 0:
                    put(step - 1, i, (lh, lu, lv))
                else:
                    here = slice(n * BLK, (n + 1) * BLK)
                    for f, (lam, x) in enumerate(((lh, h), (lu, u), (lv, v))):
                        out_ref[f, here] = lam
                        send_ref[f, here] = (
                            1.0 - step_length * defect_weight
                        ) * x - step_length * lam

    return kernel


def settle_kernel(places):
    def kernel(*refs):
        pos_ref, ends_ref, got_ref = refs[:3]
        out_ref, buffer, sems = refs[-3:]
        share = jnp.where(pos_ref[2] == 1, 1.0, step_length * defect_weight).astype(jnp.float32)
        copies = []
        at = 0
        for n, (low, height) in enumerate(places):
            here = slice(at, at + height)
            buffer[:, here] = got_ref[:, here] + share * ends_ref[:, low : low + height]
            copies.append(
                pltpu.make_async_copy(
                    buffer.at[:, pl.ds(at, height)],
                    out_ref.at[0, :, pl.ds(low, height)],
                    sems.at[n],
                )
            )
            copies[-1].start()
            at += height
        for copy in copies:
            copy.wait()

    return kernel


def gradient_kernel(
    pos_ref, start_ref, previous_ref, background_ref, near_ref, far_ref, edge_ref,
    out_ref, buffer, held, sems
):
    strip = out_ref.shape[2]

    def fill(source):
        def place(low, height, source_adj):
            here = slice(low, low + height)
            state = start_ref[:, HALO + low : HALO + low + height]
            buffer[:, here] = defect_weight * (state - source[:, here]) + source_adj

        cut = BLK + near_ref.shape[1]
        place(0, BLK, edge_ref[:, :BLK])
        place(BLK, near_ref.shape[1], near_ref[...])
        place(cut, far_ref.shape[1], far_ref[...])
        place(strip - BLK, BLK, edge_ref[:, BLK:])

    @pl.when(pos_ref[4] == 1)
    def _():
        copy = pltpu.make_async_copy(background_ref, held, sems.at[0])
        copy.start()
        copy.wait()
        fill(held)

    @pl.when(pos_ref[4] != 1)
    def _():
        fill(previous_ref)

    copy = pltpu.make_async_copy(buffer, out_ref.at[0], sems.at[1])
    copy.start()
    copy.wait()


def shifted(block, axis, distance):
    devices = range(lax.axis_size(axis))
    route = [(i - distance, i) for i in devices if i - distance in devices]
    return lax.ppermute(block, axis, route)


def local(states, background, obs_cells, obs_values, land_mask):
    strip, columns = states.shape[2], states.shape[3]
    rows = strip + 2 * HALO
    at_first = lax.axis_index("tm") == 0
    at_final = lax.axis_index("tm") == lax.axis_size("tm") - 1
    base = lax.axis_index("space") * strip - HALO
    odd = lax.axis_index("space") & 1
    pos = jnp.stack(
        [
            base,
            jnp.int32(strip) * lax.axis_size("space"),
            at_final.astype(jnp.int32),
            odd,
            at_first.astype(jnp.int32),
            ((lax.axis_index("tm") & (RING - 1) < 3) & (lax.axis_index("tm") >= RING)).astype(jnp.int32),
        ]
    ).astype(jnp.int32)
    f32 = jnp.float32

    def params(megabytes):
        return pltpu.CompilerParams(vmem_limit_bytes=megabytes * 1024 * 1024)

    def cost(us):
        return pl.CostEstimate(
            flops=int(us * 1.0e9), transcendentals=0, bytes_accessed=int(us * 3.0e6)
        )

    observed = obs_cells.shape[2]
    cut = near_blocks(strip // BLK) * BLK
    map_shapes = (
        jax.ShapeDtypeStruct((NSTEP, rows, columns), f32),
        jax.ShapeDtypeStruct((NSTEP, rows, columns), f32),
        jax.ShapeDtypeStruct((3, rows, columns), f32),
        jax.ShapeDtypeStruct((strip, columns), jnp.int32),
    )
    cross, pair, cells, values, near, far, *maps = pl.pallas_call(
        prepare_kernel,
        out_shape=(
            jax.ShapeDtypeStruct((4, HALO, columns), f32),
            jax.ShapeDtypeStruct((4, HALO, columns), f32),
            jax.ShapeDtypeStruct((NSTEP, observed), jnp.int32),
            jax.ShapeDtypeStruct((NSTEP, observed), f32),
            jax.ShapeDtypeStruct((3, cut, columns), f32),
            jax.ShapeDtypeStruct((3, strip - cut, columns), f32),
        )
        + map_shapes,
        in_specs=[smem()] + [hbm()] * 4,
        out_specs=(vmem(),) * 10,
        scratch_shapes=[
            pltpu.VMEM((2, HALO, columns), jnp.int32),
            pltpu.SemaphoreType.DMA((10,)),
        ],
        compiler_params=params(16),
        cost_estimate=cost(0.5),
        name="prepare",
    )(pos, *(off_chip(x) for x in (states, land_mask, obs_cells, obs_values)))
    cross, pair, near, far, pos, even = lax.optimization_barrier(
        (cross, pair, near, far, pos, odd == 0)
    )
    strips = lax.axis_size("space")
    inner = [(i, i ^ 1) for i in range(strips)]
    outer = [(i, j) for i in range(strips) for j in [((i + 1) ^ 1) - 1] if 0 <= j < strips]
    cross = lax.ppermute(cross, "space", outer)
    pair = lax.ppermute(pair, "space", inner)
    far = shifted(far, "tm", -1)
    near = shifted(near, "tm", -1)

    count, total, start, bits = maps
    step_shapes = (
        jax.ShapeDtypeStruct((rows, columns), f32),
        jax.ShapeDtypeStruct((3, strip, columns), f32),
    ) + (jax.ShapeDtypeStruct((3, rows, columns), f32),) * (NSTEP + 1)
    row = lax.broadcasted_iota(jnp.int32, (3, HALO, columns), 1)
    rim = jnp.where((row < HALO // 2) != even, cross[:3], pair[:3])
    steps = pl.pallas_call(
        early_kernel,
        out_shape=step_shapes,
        in_specs=[smem()] + [vmem()] * 4,
        out_specs=(vmem(),) * len(step_shapes),
        input_output_aliases={1: 2},
        compiler_params=params(24),
        cost_estimate=cost(0.01),
        name="early",
    )(pos, start, cross, pair, bits)
    rim, cross, pair, steps = lax.optimization_barrier((rim, cross, pair, steps))
    rim = shifted(rim, "tm", -1)
    held = (count, total, bits, *steps)
    count, total, bits, land, ends, *path = pl.pallas_call(
        late_kernel,
        out_shape=(map_shapes[0], map_shapes[1], map_shapes[3]) + step_shapes,
        in_specs=[smem(), vmem(), vmem(), hbm(), hbm(), vmem(), vmem()] + [vmem()] * len(held),
        out_specs=(vmem(),) * len(held),
        input_output_aliases={7 + n: n for n in range(len(held))},
        scratch_shapes=[pltpu.SemaphoreType.DMA((2,))],
        compiler_params=params(28),
        cost_estimate=cost(6),
        name="late",
    )(pos, cells, values, off_chip(states), off_chip(land_mask), cross, pair, *held)

    previous = shifted(ends, "tm", 1)

    def adjoint(part, height, *operands):
        work = jax.ShapeDtypeStruct((NSTEP, 3, rows, columns), f32)
        return pl.pallas_call(
            adjoint_kernel(part),
            out_shape=(jax.ShapeDtypeStruct((3, height, columns), f32),) * 2 + (work,),
            in_specs=[smem()] + [vmem()] * len(operands),
            out_specs=(vmem(),) * 3,
            input_output_aliases={} if part == "near" else {len(operands): 2},
            compiler_params=params(24),
            cost_estimate=cost({"near": 0.1, "far": 60, "edge": 0.5}[part]),
            name="adjoint_" + part,
        )(pos, *operands)

    shared = (land, count, total, *path)
    first, near_send, work = adjoint("near", cut - 2 * BLK, *shared, near)
    second, far_send, work = adjoint("far", strip - cut, *shared, far, work)
    outer, edge_send, work = adjoint("edge", 2 * BLK, *shared, rim, work)
    edge_sent = shifted(edge_send, "tm", -1)
    far_sent = shifted(far_send, "tm", -1)
    near_sent = shifted(near_send, "tm", -1)

    def settle(name, places, arrived, *held):
        height = arrived.shape[1]
        return pl.pallas_call(
            settle_kernel(places),
            out_shape=jax.ShapeDtypeStruct(states.shape, f32),
            in_specs=[smem()] + [vmem()] * 2 + [hbm()] * len(held),
            out_specs=hbm(),
            scratch_shapes=[
                pltpu.VMEM((3, height, columns), f32),
                pltpu.SemaphoreType.DMA((len(places),)),
            ],
            input_output_aliases={3: 0} if held else {},
            compiler_params=params(8),
            cost_estimate=cost(0.01),
            name="settle_" + name,
        )(pos, ends, arrived, *(off_chip(x) for x in held))

    gradient = pl.pallas_call(
        gradient_kernel,
        out_shape=jax.ShapeDtypeStruct(states.shape, f32),
        in_specs=[smem(), vmem(), vmem(), hbm(), vmem(), vmem(), vmem()],
        out_specs=hbm(),
        scratch_shapes=[
            pltpu.VMEM((3, strip, columns), f32),
            pltpu.VMEM((3, strip, columns), f32),
            pltpu.SemaphoreType.DMA((2,)),
        ],
        compiler_params=params(12),
        cost_estimate=cost(0.01),
        name="gradient",
    )(pos, path[0], previous, off_chip(background), first, second, outer)
    next_state = settle("near", [(BLK, cut - 2 * BLK)], near_sent)
    next_state = settle("far", [(cut - BLK, strip - cut)], far_sent, next_state, gradient)
    next_state = settle("edge", [(0, BLK), (strip - BLK, BLK)], edge_sent, next_state)
    return (gradient, next_state)


def solution(mesh):
    in_specs = (
        P("tm", None, "space", None),
        P(None, "space", None),
        P("tm", None, None),
        P("tm", None, None),
        P("space", None),
    )
    out_specs = (P("tm", None, "space", None), P("tm", None, "space", None))
    return jax.shard_map(local, mesh=mesh, in_specs=in_specs, out_specs=out_specs, check_vma=False)
```
